32 devices in a mesh: rep: 2 (over y), seq: 8 (over z, x), grp: 2 (over core).
Axes of the slice: x: 2, y: 2, z: 4, core: 2. Of those that a mesh axis runs over, the one named last changes fastest.
Arguments:
- hidden: bfloat16 [4352, 8192], P(('rep', 'seq'), 'grp'), parts along dimension 0, may hold values from -6 to 6
- proj: bfloat16 [3, 256, 8192], P(None, 'seq', 'grp'), may hold values from -0.0625 to 0.0625
- short_taps: float32 [3, 3, 256], P(None, None, 'grp'), may hold values from -4 to 4
- filters: float32 [16, 128], P('grp'), may hold values from -0.5 to 0.5
- grad_out: bfloat16 [4352, 256], P(('rep', 'seq'), 'grp'), parts along dimension 0, may hold values from -6 to 6
- var_pos: int32 [256], P(('rep', 'seq')), parts along dimension 0, may hold values from 0 to 2175, as said below
- alt_hidden: bfloat16 [256, 8192], P(('rep', 'seq'), 'grp'), parts along dimension 0, may hold values from -6 to 6
Outputs:
- attribution: float32 [4352], P(('rep', 'seq')), parts along dimension 0
- effect: float32 [256], P(('rep', 'seq')), parts along dimension 0
The draws below stay inside these ranges and needn't reach their ends.
There are 2 independent parts, one for each index of `rep`. The reference program is written for one: setup_inputs(seed, part) draws one part's arguments, and reference() takes and returns one part's arrays. A program takes and returns all parts, laid end to end along the dimension named above; an argument that names none is the same for every part. Nothing has to cross between parts.
Inputs may be any that keep to these rules, and one draw needn't show every extreme that they name: `var_pos`: variants v of block j (j * 16 <= v < (j + 1) * 16) lie in tokens j * 272 to (j + 1) * 272 - 1; each block holds the first and the last of those tokens.
All inputs are finite; a program needn't handle non-finite values.
Results may differ from the reference program's by a relative error of at most 0.0028.
Values may be sent and summed in bfloat16 or wider, within the bound.
No kernel may reach another device: no remote copies, remote signals or barrier semaphores. Data moves between devices by JAX's collectives and lax.ppermute only.
A program may use at most 64 MiB of HBM per device.

```python
import jax
import jax.numpy as jnp
from jax import lax

D = 8192
GROUP = 16
FGROUPS = 16
FLEN = 128
SHORT = 3
TOK = 272
VAR_DEV = 16
CW = 256
S = 2176
NVAR = 128
N_SEQ = 8


def draw_var_pos(key, part):
    offsets = jax.random.randint(key, (NVAR,), 0, TOK)
    slot = jnp.arange(NVAR) % VAR_DEV
    offsets = jnp.where(slot == 0, 0, jnp.where(slot == 1, TOK - 1, offsets))
    return (jnp.arange(NVAR) // VAR_DEV * TOK + offsets).astype(jnp.int32)


def shard_levels(stream_key, extent, pieces, smallest, largest):
    loudness = 1.0
    for dim, blocks in pieces:
        steps = jax.random.uniform(jax.random.fold_in(jax.random.fold_in(stream_key, 6), dim), (blocks,), jnp.float32, smallest / len(pieces), largest / len(pieces))
        loudness = loudness * jnp.repeat(jnp.exp(steps), extent[dim] // blocks).reshape((-1,) + (1,) * (len(extent) - 1 - dim))
    return loudness


def bell_draw(rng, shape, spread, reach, shards=(), kind=jnp.bfloat16):
    entries = spread * jax.random.normal(rng, shape, jnp.float32)
    if shards:
        entries = entries * shard_levels(rng, shape, shards, -0.22, 0.18)
    return jnp.clip(entries, -reach, reach).astype(kind)


def setup_inputs(seed: int = 0, part: int = 0) -> dict:
    seeds = jax.random.split(jax.random.key(seed), 8)
    part_splits = jax.random.split(jax.random.fold_in(seeds[7], part), 8)
    hidden = bell_draw(part_splits[0], (S, D), 1.0, 6.0, ((0, 8), (1, 2)))
    proj = bell_draw(seeds[1], (3, CW, D), D ** -0.5, 0.0625, ((1, 8), (2, 2)))
    short_taps = bell_draw(seeds[2], (SHORT, 3, CW), 0.6, 4.0, ((2, 2),), jnp.float32)
    filters = bell_draw(seeds[3], (FGROUPS, FLEN), FLEN ** -0.5, 0.5, ((0, 2),), jnp.float32)
    grad_out = bell_draw(part_splits[4], (S, CW), 1.0, 6.0, ((0, 8), (1, 2)))
    var_pos = draw_var_pos(jax.random.fold_in(jax.random.fold_in(seeds[7], part), 71), part)
    alt_hidden = bell_draw(part_splits[6], (NVAR, D), 1.0, 6.0, ((0, 8), (1, 2)))
    return {"hidden": hidden, "proj": proj, "short_taps": short_taps, "filters": filters, "grad_out": grad_out, "var_pos": var_pos, "alt_hidden": alt_hidden}


def causal_taps(source, taps):
    tap_count = taps.shape[0]
    row_count = source.shape[0]
    padded = jnp.concatenate([jnp.zeros((tap_count - 1,) + source.shape[1:], jnp.float32), source], 0)
    summed = jnp.zeros(source.shape, jnp.float32)
    for offset in range(tap_count):
        begin = tap_count - 1 - offset
        summed = summed + taps[offset] * padded[begin:begin + row_count]
    return summed


def later_taps(source, taps):
    tap_count = taps.shape[0]
    row_count = source.shape[0]
    padded = jnp.concatenate([source, jnp.zeros((tap_count - 1,) + source.shape[1:], jnp.float32)], 0)
    summed = jnp.zeros(source.shape, jnp.float32)
    for offset in range(tap_count):
        summed = summed + taps[offset] * padded[offset:offset + row_count]
    return summed


def long_filter(source, filters, later):
    row_count = source.shape[0]
    per_channel = jnp.repeat(filters.astype(jnp.float32), GROUP, axis=0).T
    zero_rim = jnp.zeros((FLEN - 1, source.shape[1]), jnp.float32)
    if later:
        padded = jnp.concatenate([source, zero_rim], 0)
    else:
        padded = jnp.concatenate([zero_rim, source], 0)

    def accumulate(offset, summed):
        begin = offset if later else FLEN - 1 - offset
        section = lax.dynamic_slice_in_dim(padded, begin, row_count, 0)
        return summed + lax.dynamic_index_in_dim(per_channel, offset, 0, keepdims=False) * section

    return lax.fori_loop(0, FLEN, accumulate, jnp.zeros(source.shape, jnp.float32))


def reference(hidden, proj, short_taps, filters, grad_out, var_pos, alt_hidden):
    weights = proj.astype(jnp.float32)

    def featurize(block_rows):
        return jnp.einsum('td,fcd->tfc', block_rows.astype(jnp.float32), weights)

    feature = lax.map(featurize, hidden.reshape(N_SEQ, TOK, D)).reshape(N_SEQ * TOK, 3, CW)
    mixed = causal_taps(feature, short_taps)
    queries = mixed[:, 0]
    keys_part = mixed[:, 1]
    values_part = mixed[:, 2]
    product = keys_part * values_part
    filtered = long_filter(product, filters, False)
    upstream = grad_out.astype(jnp.float32)
    back_queries = upstream * filtered
    back_filtered = upstream * queries
    back_product = long_filter(back_filtered, filters, True)
    back_mixed = jnp.stack([back_queries, back_product * values_part, back_product * keys_part], 1)
    back_feature = later_taps(back_mixed, short_taps).astype(jnp.bfloat16)
    factor = D ** -0.5

    def scoring(section):
        back_block, block_rows, positions, alternates, block_index = section
        back_hidden = jnp.einsum('tfc,fcd->td', back_block.astype(jnp.float32), weights)
        rows_float = block_rows.astype(jnp.float32)
        attribution = jnp.sum(back_hidden * rows_float, 1) * factor
        local_rows = (positions - block_index * TOK).astype(jnp.int32)
        picked = jnp.take(back_hidden, local_rows, axis=0)
        present = jnp.take(rows_float, local_rows, axis=0)
        change = alternates.astype(jnp.float32) - present
        return attribution, jnp.sum(picked * change, 1) * factor

    attribution, effect = lax.map(scoring, (back_feature.reshape(N_SEQ, TOK, 3, CW), hidden.reshape(N_SEQ, TOK, D), var_pos.reshape(N_SEQ, VAR_DEV), alt_hidden.reshape(N_SEQ, VAR_DEV, D), jnp.arange(N_SEQ, dtype=jnp.int32)))
    return attribution.reshape(-1), effect.reshape(-1)
```

```python
import jax
import jax.numpy as jnp
from jax import lax
from jax.experimental import pallas as pl
from jax.experimental.pallas import tpu as pltpu
from jax.sharding import PartitionSpec as P

D = 8192
GROUP = 16
EDGE = 8


def shifted(block, axis, distance):
    devices = range(lax.axis_size(axis))
    route = [(i - distance, i) for i in devices if i - distance in devices]
    return lax.ppermute(block, axis, route)


def swapped(block, axis):
    return lax.ppermute(block, axis, [(0, 1), (1, 0)])


def mixer_kernel(
    rows, reach, picks, feature, before, after, grad, grad_after, taps, filters, out,
    query, key, value, product, back_filtered, grads, summed,
):
    span = filters.shape[0]
    variants = picks.shape[0]
    ahead = rows + EDGE
    query[:EDGE] = before[2 * reach :]
    query[EDGE : EDGE + rows] = feature[0, :rows]
    query[EDGE + rows :] = after[:reach]
    for index, extended in ((1, key), (2, value)):
        extended[:reach] = before[(index - 1) * reach : index * reach]
        extended[reach : reach + rows] = feature[index, :rows]
        extended[reach + rows :] = after[reach + (index - 1) * EDGE : reach + index * EDGE]

    def tap(offset, index):
        return taps[offset * 3 + index : offset * 3 + index + 1, :]

    def mixed(extended, index, begin, count):
        total = tap(0, index) * extended[begin : begin + count]
        for offset in (1, 2):
            total = total + tap(offset, index) * extended[begin - offset : begin - offset + count]
        return total

    shift = reach - span
    product[...] = mixed(key, 1, shift, span + ahead) * mixed(value, 2, shift, span + ahead)
    back_filtered[:rows] = grad[...].astype(jnp.float32) * mixed(query, 0, EDGE, rows)
    back_filtered[rows:] = grad_after[...].astype(jnp.float32) * mixed(
        query, 0, EDGE + rows, reach
    )

    def long_filter(source, later):
        def accumulate(block, total):
            for inner in range(8):
                offset = block * 8 + inner
                begin = offset if later else span - offset
                total = total + filters[pl.ds(offset, 1), :] * source[pl.ds(begin, ahead), :]
            return total

        return lax.fori_loop(
            0, span // 8, accumulate, jnp.zeros((ahead, filters.shape[1]), jnp.float32)
        )

    filtered = long_filter(product, False)
    grads[0, :rows] = grad[...].astype(jnp.float32) * filtered[:rows]
    grads[0, rows:] = grad_after[:EDGE].astype(jnp.float32) * filtered[rows:]
    back_product = long_filter(back_filtered, True)
    grads[1] = back_product * mixed(value, 2, reach, ahead)
    grads[2] = back_product * mixed(key, 1, reach, ahead)
    total = jnp.zeros((rows, filters.shape[1]), jnp.float32)
    for index in range(3):
        back = tap(0, index) * grads[index, :rows]
        for offset in (1, 2):
            back = back + tap(offset, index) * grads[index, offset : offset + rows]
        back = back.astype(jnp.bfloat16).astype(jnp.float32)
        grads[index, :rows] = back
        total = total + back * feature[index, :rows]
    summed[:rows] = total
    for variant in range(variants):
        at = picks[variant]
        change = jnp.zeros((1, filters.shape[1]), jnp.float32)
        for index in range(3):
            alternate = feature[index, rows + variant : rows + variant + 1]
            present = feature[index, pl.ds(at, 1)]
            change = change + grads[index, pl.ds(at, 1)] * (alternate - present)
        summed[rows + variant : rows + variant + 1] = change
    out[...] = lax.dot_general(
        jnp.ones((8, filters.shape[1]), jnp.float32),
        summed[...],
        (((1,), (1,)), ((), ())),
        precision=lax.Precision.HIGHEST,
        preferred_element_type=jnp.float32,
    )


def mixer(picks, feature, before, after, grad, grad_after, taps, filters):
    rows, lanes = grad.shape
    reach = grad_after.shape[0]
    span = filters.shape[0]
    count = feature.shape[1]

    def body(*refs):
        mixer_kernel(rows, reach, *refs)

    vmem = pl.BlockSpec(memory_space=pltpu.VMEM)
    return pl.pallas_call(
        body,
        out_shape=jax.ShapeDtypeStruct((8, count), jnp.float32),
        in_specs=[pl.BlockSpec(memory_space=pltpu.SMEM)] + [vmem] * 7,
        out_specs=vmem,
        scratch_shapes=[
            pltpu.VMEM((EDGE + rows + reach, lanes), jnp.float32),
            pltpu.VMEM((reach + rows + EDGE, lanes), jnp.float32),
            pltpu.VMEM((reach + rows + EDGE, lanes), jnp.float32),
            pltpu.VMEM((span + rows + EDGE, lanes), jnp.float32),
            pltpu.VMEM((rows + reach, lanes), jnp.float32),
            pltpu.VMEM((3, rows + EDGE, lanes), jnp.float32),
            pltpu.VMEM((count, lanes), jnp.float32),
        ],
        name="mixer",
    )(picks, feature, before, after, grad, grad_after, taps, filters)


def per_device(hidden, proj, short_taps, filters, grad_out, var_pos, alt_hidden):
    rows = hidden.shape[0]
    lanes = grad_out.shape[1]
    reach = filters.shape[1] + EDGE
    rep, half = lax.axis_index("rep"), lax.axis_index("grp")
    parts = lax.axis_size("rep")
    width = hidden.shape[1] // parts

    tokens = jnp.concatenate([hidden, alt_hidden], 0)
    theirs = swapped(lax.dynamic_slice_in_dim(tokens, (1 - rep) * width, width, 1), "rep")
    panels = lax.all_gather(
        lax.dynamic_slice_in_dim(proj, rep * width, width, 2), "seq", axis=1, tiled=True
    )
    ours = lax.dynamic_slice_in_dim(tokens, rep * width, width, 1)
    grad_after = shifted(grad_out[:reach], "seq", -1)
    per_channel = jnp.repeat(filters, GROUP, axis=0).T
    picks = var_pos - lax.axis_index("seq") * rows

    both = jnp.concatenate([ours, theirs], 0)
    partial = jnp.einsum("td,fcd->ftc", both, panels, preferred_element_type=jnp.float32)
    keep = lax.dynamic_slice_in_dim(partial, half * lanes, lanes, 2)
    give = lax.dynamic_slice_in_dim(partial, (1 - half) * lanes, lanes, 2)
    chip = keep + swapped(give, "grp")
    count = tokens.shape[0]
    feature = chip[:, :count] + swapped(chip[:, count:], "rep")

    before = shifted(
        jnp.concatenate(
            [
                feature[1, rows - reach : rows],
                feature[2, rows - reach : rows],
                feature[0, rows - EDGE : rows],
            ],
            0,
        ),
        "seq",
        1,
    )
    after = shifted(
        jnp.concatenate([feature[0, :reach], feature[1, :EDGE], feature[2, :EDGE]], 0), "seq", -1
    )
    scores = mixer(
        picks, feature, before, after, grad_out, grad_after,
        short_taps.reshape(9, lanes), per_channel,
    )[0]
    scores = lax.psum(scores, "grp") * D ** (-0.5)
    return scores[:rows], scores[rows:]


def solution(mesh):
    in_specs = (
        P(("rep", "seq"), "grp"),
        P(None, "seq", "grp"),
        P(None, None, "grp"),
        P("grp", None),
        P(("rep", "seq"), "grp"),
        P(("rep", "seq")),
        P(("rep", "seq"), "grp"),
    )
    out_specs = (P(("rep", "seq")), P(("rep", "seq")))
    return jax.shard_map(
        per_device, mesh=mesh, in_specs=in_specs, out_specs=out_specs, check_vma=False
    )
```

```python
import jax
import jax.numpy as jnp
from jax import lax
from jax.experimental import pallas as pl
from jax.experimental.pallas import tpu as pltpu
from jax.sharding import PartitionSpec as P

D = 8192
GROUP = 16
EDGE = 8
AXES = ("rep", "seq", "grp")
VMEM = pl.BlockSpec(memory_space=pltpu.VMEM)
SMEM = pl.BlockSpec(memory_space=pltpu.SMEM)


def shifted(block, axis, distance):
    devices = range(lax.axis_size(axis))
    route = [(i - distance, i) for i in devices if i - distance in devices]
    return lax.ppermute(block, axis, route)


def crossed(block, axis, bit):
    return lax.ppermute(block, axis, [(i, i ^ bit) for i in range(lax.axis_size(axis))])


def routed(block, target):
    parts, members, cores = (lax.axis_size(axis) for axis in AXES)
    route = []
    for rep in range(parts):
        for seq in range(members):
            for core in range(cores):
                goal = target(rep, seq, core)
                if goal is not None:
                    source = (rep * members + seq) * cores + core
                    route.append((source, (goal[0] * members + goal[1]) * cores + goal[2]))
    return lax.ppermute(block, AXES, route)


def product_kernel(place, ours, theirs, first, second, third, fourth, out, panel):
    kinds, height, _ = first.shape
    lanes = 4 * height
    count = ours.shape[0]
    for number, block in enumerate((first, second, third, fourth)):
        begin = pl.multiple_of((place[0] ^ number) * height, height)
        for kind in range(kinds):
            panel[pl.ds(kind * lanes + begin, height), :] = block[kind]
    for index, tokens in enumerate((ours, theirs)):
        result = lax.dot_general(
            tokens[...],
            panel[...],
            (((1,), (1,)), ((), ())),
            preferred_element_type=jnp.float32,
        )
        for kind in range(kinds):
            out[kind, index * count : (index + 1) * count] = result[
                :, kind * lanes : (kind + 1) * lanes
            ]


def product(place, ours, theirs, blocks):
    kinds, height, width = blocks[0].shape
    count = ours.shape[0]
    return pl.pallas_call(
        product_kernel,
        out_shape=jax.ShapeDtypeStruct((kinds, 2 * count, 4 * height), jnp.float32),
        in_specs=[SMEM] + [VMEM] * 6,
        out_specs=VMEM,
        scratch_shapes=[pltpu.VMEM((kinds * 4 * height, width), jnp.bfloat16)],
        compiler_params=pltpu.CompilerParams(vmem_limit_bytes=24 << 20),
        cost_estimate=pl.CostEstimate(
            flops=2 * 2 * count * kinds * 4 * height * width,
            bytes_accessed=2 * 2 * count * width + 8 * kinds * height * width,
            transcendentals=0,
        ),
        name="product",
    )(place, ours, theirs, *blocks)


def mixer_kernel(
    rows, reach, picks, feature, before, after, grad, grad_after, taps, filters, out,
    query, key, value, product, back_filtered, grads, summed,
):
    span = filters.shape[0]
    variants = picks.shape[0]
    ahead = rows + EDGE
    query[:EDGE] = before[2 * reach :]
    query[EDGE : EDGE + rows] = feature[0, :rows]
    query[EDGE + rows :] = after[:reach]
    for index, extended in ((1, key), (2, value)):
        extended[:reach] = before[(index - 1) * reach : index * reach]
        extended[reach : reach + rows] = feature[index, :rows]
        extended[reach + rows :] = after[reach + (index - 1) * EDGE : reach + index * EDGE]

    def tap(offset, index):
        return taps[offset * 3 + index : offset * 3 + index + 1, :]

    def mixed(extended, index, begin, count):
        total = tap(0, index) * extended[begin : begin + count]
        for offset in (1, 2):
            total = total + tap(offset, index) * extended[begin - offset : begin - offset + count]
        return total

    shift = reach - span
    product[...] = mixed(key, 1, shift, span + ahead) * mixed(value, 2, shift, span + ahead)
    back_filtered[:rows] = grad[...].astype(jnp.float32) * mixed(query, 0, EDGE, rows)
    back_filtered[rows:] = grad_after[...].astype(jnp.float32) * mixed(
        query, 0, EDGE + rows, reach
    )

    def long_filter(source, later):
        def accumulate(block, total):
            for inner in range(8):
                offset = block * 8 + inner
                begin = offset if later else span - offset
                total = total + filters[pl.ds(offset, 1), :] * source[pl.ds(begin, ahead), :]
            return total

        return lax.fori_loop(
            0, span // 8, accumulate, jnp.zeros((ahead, filters.shape[1]), jnp.float32)
        )

    filtered = long_filter(product, False)
    grads[0, :rows] = grad[...].astype(jnp.float32) * filtered[:rows]
    grads[0, rows:] = grad_after[:EDGE].astype(jnp.float32) * filtered[rows:]
    back_product = long_filter(back_filtered, True)
    grads[1] = back_product * mixed(value, 2, reach, ahead)
    grads[2] = back_product * mixed(key, 1, reach, ahead)
    total = jnp.zeros((rows, filters.shape[1]), jnp.float32)
    for index in range(3):
        back = tap(0, index) * grads[index, :rows]
        for offset in (1, 2):
            back = back + tap(offset, index) * grads[index, offset : offset + rows]
        back = back.astype(jnp.bfloat16).astype(jnp.float32)
        grads[index, :rows] = back
        total = total + back * feature[index, :rows]
    summed[:rows] = total
    for variant in range(variants):
        at = picks[variant]
        change = jnp.zeros((1, filters.shape[1]), jnp.float32)
        for index in range(3):
            alternate = feature[index, rows + variant : rows + variant + 1]
            present = feature[index, pl.ds(at, 1)]
            change = change + grads[index, pl.ds(at, 1)] * (alternate - present)
        summed[rows + variant : rows + variant + 1] = change
    out[...] = lax.dot_general(
        jnp.ones((8, filters.shape[1]), jnp.float32),
        summed[...],
        (((1,), (1,)), ((), ())),
        precision=lax.Precision.HIGHEST,
        preferred_element_type=jnp.float32,
    )


def mixer(picks, feature, before, after, grad, grad_after, taps, filters):
    rows, lanes = grad.shape
    reach = grad_after.shape[0]
    span = filters.shape[0]
    count = feature.shape[1]

    def body(*refs):
        mixer_kernel(rows, reach, *refs)

    return pl.pallas_call(
        body,
        out_shape=jax.ShapeDtypeStruct((8, count), jnp.float32),
        in_specs=[SMEM] + [VMEM] * 7,
        out_specs=VMEM,
        scratch_shapes=[
            pltpu.VMEM((EDGE + rows + reach, lanes), jnp.float32),
            pltpu.VMEM((reach + rows + EDGE, lanes), jnp.float32),
            pltpu.VMEM((reach + rows + EDGE, lanes), jnp.float32),
            pltpu.VMEM((span + rows + EDGE, lanes), jnp.float32),
            pltpu.VMEM((rows + reach, lanes), jnp.float32),
            pltpu.VMEM((3, rows + EDGE, lanes), jnp.float32),
            pltpu.VMEM((count, lanes), jnp.float32),
        ],
        name="mixer",
    )(picks, feature, before, after, grad, grad_after, taps, filters)


def gathered_features(tokens, proj, lanes):
    rep, half = lax.axis_index("rep"), lax.axis_index("grp")
    width = proj.shape[2] // lax.axis_size("rep")
    count = sum(piece.shape[0] for piece in tokens)

    def columns(side):
        return jnp.concatenate(
            [lax.dynamic_slice_in_dim(piece, side * width, width, 1) for piece in tokens], 0
        )

    theirs = crossed(columns(1 - rep), "rep", 1)
    panels = lax.all_gather(
        lax.dynamic_slice_in_dim(proj, rep * width, width, 2), "seq", axis=1, tiled=True
    )
    both = jnp.concatenate([columns(rep), theirs], 0)
    partial = jnp.einsum("td,fcd->ftc", both, panels, preferred_element_type=jnp.float32)
    keep = lax.dynamic_slice_in_dim(partial, half * lanes, lanes, 2)
    give = lax.dynamic_slice_in_dim(partial, (1 - half) * lanes, lanes, 2)
    chip = keep + crossed(give, "grp", 1)
    return chip[:, :count] + crossed(chip[:, count:], "rep", 1)


def cube_features(tokens, proj):
    rep, seq, half = (lax.axis_index(axis) for axis in AXES)
    width = proj.shape[2] // lax.axis_size("rep")
    count = sum(piece.shape[0] for piece in tokens)
    bar = lax.optimization_barrier

    def columns(side):
        return jnp.concatenate(
            [lax.dynamic_slice_in_dim(piece, side * width, width, 1) for piece in tokens], 0
        )

    own = lax.dynamic_slice_in_dim(proj, rep * width, width, 2)
    own_2 = crossed(own, "seq", 2)
    own_4 = crossed(own, "seq", 4)
    own_1 = crossed(own, "seq", 1)
    theirs = crossed(columns(1 - rep), "rep", 1)
    own_2, own_1 = bar((own_2, own_1))
    own_3 = crossed(own_2, "seq", 1)
    own_4, own_3 = bar((own_4, own_3))
    own_6 = crossed(own_4, "seq", 2)
    own_5 = crossed(own_4, "seq", 1)
    own_6, own_5 = bar((own_6, own_5))
    cut = own.shape[1] // 2
    own_7 = jnp.concatenate(
        [crossed(own_6[:, :cut], "seq", 1), crossed(own_5[:, cut:], "seq", 2)], 1
    )
    ours = columns(rep)
    place = (seq % 4).reshape(1)

    def chip_sum(partial, near):
        keeper = lambda seq, core: (core == seq // 4) == near
        brought = routed(
            partial, lambda rep, seq, core: None if keeper(seq, core) else (rep, seq, 1 - core)
        )
        summed = partial + brought
        other = routed(
            summed[:, count:],
            lambda rep, seq, core: (1 - rep, seq, core) if keeper(seq, core) else None,
        )
        return summed[:, :count] + other

    near = chip_sum(product(place, ours, theirs, (own, own_1, own_2, own_3)), True)
    far = chip_sum(product(place, ours, theirs, (own_4, own_5, own_6, own_7)), False)
    return jnp.where(half == seq // 4, near, far)


def per_device(hidden, proj, short_taps, filters, grad_out, var_pos, alt_hidden):
    rows = hidden.shape[0]
    lanes = grad_out.shape[1]
    reach = filters.shape[1] + EDGE
    grad_after = shifted(grad_out[:reach], "seq", -1)
    per_channel = jnp.repeat(filters, GROUP, axis=0).T
    picks = var_pos - lax.axis_index("seq") * rows
    if lax.axis_size("seq") == 8:
        feature = cube_features((hidden, alt_hidden), proj)
    else:
        feature = gathered_features((hidden, alt_hidden), proj, lanes)
    before = shifted(
        jnp.concatenate(
            [
                feature[1, rows - reach : rows],
                feature[2, rows - reach : rows],
                feature[0, rows - EDGE : rows],
            ],
            0,
        ),
        "seq",
        1,
    )
    after = shifted(
        jnp.concatenate([feature[0, :reach], feature[1, :EDGE], feature[2, :EDGE]], 0), "seq", -1
    )
    scores = mixer(
        picks, feature, before, after, grad_out, grad_after,
        short_taps.reshape(9, lanes), per_channel,
    )[0]
    scores = lax.psum(scores, "grp") * D ** (-0.5)
    return scores[:rows], scores[rows:]


def solution(mesh):
    in_specs = (
        P(("rep", "seq"), "grp"),
        P(None, "seq", "grp"),
        P(None, None, "grp"),
        P("grp", None),
        P(("rep", "seq"), "grp"),
        P(("rep", "seq")),
        P(("rep", "seq"), "grp"),
    )
    out_specs = (P(("rep", "seq")), P(("rep", "seq")))
    return jax.shard_map(
        per_device, mesh=mesh, in_specs=in_specs, out_specs=out_specs, check_vma=False
    )
```

```python
import jax
import jax.numpy as jnp
from jax import lax
from jax.experimental import pallas as pl
from jax.experimental.pallas import tpu as pltpu
from jax.sharding import PartitionSpec as P

D = 8192
GROUP = 16
EDGE = 8
PIECES = 2
AXES = ("rep", "seq", "grp")
VMEM = pl.BlockSpec(memory_space=pltpu.VMEM)
ANY = pl.BlockSpec(memory_space=pl.ANY)
HBM = pl.BlockSpec(memory_space=pltpu.HBM)
SMEM = pl.BlockSpec(memory_space=pltpu.SMEM)


def shifted(block, axis, distance):
    devices = range(lax.axis_size(axis))
    route = [(i - distance, i) for i in devices if i - distance in devices]
    return lax.ppermute(block, axis, route)


def crossed(block, axis, bit):
    return lax.ppermute(block, axis, [(i, i ^ bit) for i in range(lax.axis_size(axis))])


def moved(pairs, sems):
    copies = [
        pltpu.make_async_copy(source, target, sems.at[index])
        for index, (source, target) in enumerate(pairs)
    ]
    for copy in copies:
        copy.start()
    return copies


def part(side, width):
    return pl.ds(pl.multiple_of(side * width, width), width)


def prepare_kernel(proj, tokens, alternates, own, first, second, theirs, sems):
    width = own.shape[2]
    cut = first.shape[1]
    rows = tokens.shape[0]
    rep = lax.axis_index("rep")
    home, away = part(rep, width), part(1 - rep, width)
    step = rows // PIECES
    copies = moved(
        [
            (proj.at[:, :, home], own),
            (proj.at[:, :cut, home], first),
            (proj.at[:, cut:, home], second),
            (alternates.at[:, away], theirs.at[rows:]),
        ]
        + [
            (tokens.at[begin : begin + step, away], theirs.at[begin : begin + step])
            for begin in range(0, rows, step)
        ],
        sems,
    )
    for copy in copies:
        copy.wait()


def prepare(proj, tokens, alternates, width):
    kinds, height, _ = proj.shape
    count = tokens.shape[0] + alternates.shape[0]
    shapes = [(kinds, height, width)] + [(kinds, height // 2, width)] * 2
    shapes += [(count, width)]
    return pl.pallas_call(
        prepare_kernel,
        out_shape=[jax.ShapeDtypeStruct(shape, proj.dtype) for shape in shapes],
        in_specs=[ANY] * 3,
        out_specs=[VMEM] * 4,
        scratch_shapes=[pltpu.SemaphoreType.DMA((4 + PIECES,))],
        compiler_params=pltpu.CompilerParams(vmem_limit_bytes=60 << 20),
        name="prepare",
    )(proj, tokens, alternates)


def dots(tokens, panel, give, keep):
    kinds, _, lanes = give.shape
    size = kinds * lanes
    for begin, out in ((size, give), (0, keep)):
        result = lax.dot_general(
            tokens[...],
            panel[begin : begin + size],
            (((1,), (1,)), ((), ())),
            preferred_element_type=jnp.float32,
        )
        for kind in range(kinds):
            out[kind] = result[:, kind * lanes : (kind + 1) * lanes]


def theirs_kernel(theirs, *refs):
    blocks, (give, keep, panel) = refs[:-3], refs[-3:]
    kinds, _, lanes = give.shape
    quarter = lanes // 4
    seq = lax.axis_index("seq")
    swap = lax.axis_index("grp") ^ (seq // 4)
    done = 0
    for block in blocks:
        height = block.shape[1]
        order = done // quarter
        side = ((order // 4) ^ swap) * kinds * lanes
        at = ((seq % 4) ^ (order % 4)) * quarter + done % quarter
        for kind in range(kinds):
            panel[pl.ds(pl.multiple_of(side + kind * lanes + at, 16), height), :] = block[kind]
        done += height
    dots(theirs, panel, give, keep)


def ours_kernel(tokens, alternates, panel, give, keep, ours, sems):
    rows = tokens.shape[0]
    home = part(lax.axis_index("rep"), ours.shape[1])
    copies = moved(
        [(tokens.at[:, home], ours.at[:rows]), (alternates.at[:, home], ours.at[rows:])], sems
    )
    for copy in copies:
        copy.wait()
    dots(ours, panel, give, keep)


def products(tokens, alternates, theirs, blocks):
    count, width = theirs.shape
    kinds = blocks[0].shape[0]
    lanes = sum(block.shape[1] for block in blocks) // 2
    half = jax.ShapeDtypeStruct((kinds, count, lanes), jnp.float32)
    params = pltpu.CompilerParams(vmem_limit_bytes=10 << 20)
    cost = pl.CostEstimate(
        flops=4 * count * kinds * lanes * width,
        bytes_accessed=2 * width * (count + 2 * kinds * lanes) + 8 * kinds * count * lanes,
        transcendentals=0,
    )
    give_other, keep_other, panel = pl.pallas_call(
        theirs_kernel,
        out_shape=[half, half, jax.ShapeDtypeStruct((2 * kinds * lanes, width), theirs.dtype)],
        in_specs=[VMEM] * (1 + len(blocks)),
        out_specs=[VMEM] * 3,
        compiler_params=params,
        cost_estimate=cost,
        name="theirs",
    )(theirs, *blocks)
    give_mine, keep_mine = pl.pallas_call(
        ours_kernel,
        out_shape=[half, half],
        in_specs=[ANY, ANY, VMEM],
        out_specs=[VMEM] * 2,
        scratch_shapes=[pltpu.VMEM((count, width), theirs.dtype), pltpu.SemaphoreType.DMA((2,))],
        compiler_params=params,
        cost_estimate=cost,
        name="ours",
    )(tokens, alternates, panel)
    return give_other, keep_other, give_mine, keep_mine


def spread_kernel(filters, out):
    groups, lanes = filters.shape[0], out.shape[1]
    row = lax.broadcasted_iota(jnp.int32, (groups, lanes), 0)
    lane = lax.broadcasted_iota(jnp.int32, (groups, lanes), 1)
    out[...] = lax.dot_general(
        filters[...],
        jnp.where(lane // GROUP == row, 1.0, 0.0),
        (((0,), (0,)), ((), ())),
        precision=lax.Precision.HIGHEST,
        preferred_element_type=jnp.float32,
    )


def spread(filters):
    groups, span = filters.shape
    return pl.pallas_call(
        spread_kernel,
        out_shape=jax.ShapeDtypeStruct((span, groups * GROUP), jnp.float32),
        in_specs=[VMEM],
        out_specs=VMEM,
        compiler_params=pltpu.CompilerParams(vmem_limit_bytes=2 << 20),
        name="spread",
    )(filters)


def mixer_kernel(
    rows, reach, picks, feature, before, after, grad, taps, filters, out, effects,
    query, key, value, product, back_filtered, grads, summed,
):
    span = filters.shape[0]
    variants = picks.shape[0]
    first = lax.axis_index("seq") * rows
    ahead = rows + EDGE
    query[:EDGE] = before[2 * reach :]
    query[EDGE : EDGE + rows] = feature[0, :rows]
    query[EDGE + rows :] = after[:reach]
    for index, extended in ((1, key), (2, value)):
        extended[:reach] = before[(index - 1) * reach : index * reach]
        extended[reach : reach + rows] = feature[index, :rows]
        extended[reach + rows :] = after[reach + (index - 1) * EDGE : reach + index * EDGE]

    def tap(offset, index):
        return taps[offset, index : index + 1, :]

    def mixed(extended, index, begin, count):
        total = tap(0, index) * extended[begin : begin + count]
        for offset in (1, 2):
            total = total + tap(offset, index) * extended[begin - offset : begin - offset + count]
        return total

    shift = reach - span
    product[...] = mixed(key, 1, shift, span + ahead) * mixed(value, 2, shift, span + ahead)
    back_filtered[:rows] = grad[...].astype(jnp.float32) * mixed(query, 0, EDGE, rows)
    back_filtered[rows:] = after[reach + 2 * EDGE :] * mixed(query, 0, EDGE + rows, reach)

    def long_filter(source, later):
        def accumulate(block, total):
            for inner in range(8):
                offset = block * 8 + inner
                begin = offset if later else span - offset
                total = total + filters[pl.ds(offset, 1), :] * source[pl.ds(begin, ahead), :]
            return total

        return lax.fori_loop(
            0, span // 8, accumulate, jnp.zeros((ahead, filters.shape[1]), jnp.float32)
        )

    filtered = long_filter(product, False)
    grads[0, :rows] = grad[...].astype(jnp.float32) * filtered[:rows]
    grads[0, rows:] = after[reach + 2 * EDGE : reach + 3 * EDGE] * filtered[rows:]
    back_product = long_filter(back_filtered, True)
    grads[1] = back_product * mixed(value, 2, reach, ahead)
    grads[2] = back_product * mixed(key, 1, reach, ahead)
    total = jnp.zeros((rows, filters.shape[1]), jnp.float32)
    for index in range(3):
        back = tap(0, index) * grads[index, :rows]
        for offset in (1, 2):
            back = back + tap(offset, index) * grads[index, offset : offset + rows]
        back = back.astype(jnp.bfloat16).astype(jnp.float32)
        grads[index, :rows] = back
        total = total + back * feature[index, :rows]
    summed[:rows] = total
    for variant in range(variants):
        at = picks[variant] - first
        change = jnp.zeros((1, filters.shape[1]), jnp.float32)
        for index in range(3):
            alternate = feature[index, rows + variant : rows + variant + 1]
            present = feature[index, pl.ds(at, 1)]
            change = change + grads[index, pl.ds(at, 1)] * (alternate - present)
        summed[rows + variant : rows + variant + 1] = change
    scores = lax.dot_general(
        jnp.full((8, filters.shape[1]), 1.0, jnp.float32),
        summed[...],
        (((1,), (1,)), ((), ())),
        precision=lax.Precision.HIGHEST,
        preferred_element_type=jnp.float32,
    )
    scores = scores * D ** (-0.5)
    out[...] = scores[0, :rows]
    effects[...] = scores[0, rows:]


def mixer(picks, feature, before, after, grad, taps, filters):
    rows, lanes = grad.shape
    span = filters.shape[0]
    reach = span + EDGE
    count = feature.shape[1]

    def body(*refs):
        mixer_kernel(rows, reach, *refs)

    return pl.pallas_call(
        body,
        out_shape=[
            jax.ShapeDtypeStruct((rows,), jnp.float32),
            jax.ShapeDtypeStruct((count - rows,), jnp.float32),
        ],
        in_specs=[SMEM] + [VMEM] * 6,
        out_specs=[VMEM, VMEM],
        scratch_shapes=[
            pltpu.VMEM((EDGE + rows + reach, lanes), jnp.float32),
            pltpu.VMEM((reach + rows + EDGE, lanes), jnp.float32),
            pltpu.VMEM((reach + rows + EDGE, lanes), jnp.float32),
            pltpu.VMEM((span + rows + EDGE, lanes), jnp.float32),
            pltpu.VMEM((rows + reach, lanes), jnp.float32),
            pltpu.VMEM((3, rows + EDGE, lanes), jnp.float32),
            pltpu.VMEM((count, lanes), jnp.float32),
        ],
        compiler_params=pltpu.CompilerParams(vmem_limit_bytes=8 << 20),
        name="mixer",
    )(picks, feature, before, after, grad, taps, filters)


def gathered_features(tokens, proj, lanes):
    rep, half = lax.axis_index("rep"), lax.axis_index("grp")
    width = proj.shape[2] // lax.axis_size("rep")
    count = sum(piece.shape[0] for piece in tokens)

    def columns(side):
        return jnp.concatenate(
            [lax.dynamic_slice_in_dim(piece, side * width, width, 1) for piece in tokens], 0
        )

    theirs = crossed(columns(1 - rep), "rep", 1)
    panels = lax.all_gather(
        lax.dynamic_slice_in_dim(proj, rep * width, width, 2), "seq", axis=1, tiled=True
    )
    both = jnp.concatenate([columns(rep), theirs], 0)
    partial = jnp.einsum("td,fcd->ftc", both, panels, preferred_element_type=jnp.float32)
    keep = lax.dynamic_slice_in_dim(partial, half * lanes, lanes, 2)
    give = lax.dynamic_slice_in_dim(partial, (1 - half) * lanes, lanes, 2)
    chip = keep + crossed(give, "grp", 1)
    return chip[:, :count] + crossed(chip[:, count:], "rep", 1)


def cube_features(tokens, alternates, proj, early):
    width = proj.shape[2] // lax.axis_size("rep")
    bar = lax.optimization_barrier

    own, own_a, own_b, theirs = prepare(proj, tokens, alternates, width)
    own_4a = crossed(own_a, "seq", 4)
    own_4b = crossed(own_b, "seq", 4)
    own_2 = crossed(own, "seq", 2)
    own_1 = crossed(own, "seq", 1)
    theirs = crossed(theirs, "rep", 1)
    own_2, own_1, own_4a = bar((own_2, own_1, own_4a))
    own_3 = crossed(own_2, "seq", 1)
    own_4a, own_4b, own_3, early = bar((own_4a, own_4b, own_3, early))
    own_6a = crossed(own_4a, "seq", 2)
    own_6b = crossed(own_4b, "seq", 2)
    own_5b = crossed(own_4b, "seq", 1)
    own_5a = crossed(own_4a, "seq", 1)
    own_6a, own_6b, own_5a, own_5b = bar((own_6a, own_6b, own_5a, own_5b))
    own_7a = crossed(own_6a, "seq", 1)
    own_7b = crossed(own_5b, "seq", 2)

    near = own, own_1, own_2, own_3
    far = own_4a, own_4b, own_5a, own_5b, own_6a, own_6b, own_7a, own_7b
    give_other, keep_other, give_mine, keep_mine = products(tokens, alternates, theirs, near + far)
    other = crossed(keep_other + crossed(give_other, "grp", 1), "rep", 1)
    return keep_mine + crossed(give_mine, "grp", 1) + other, early


def per_device(hidden, proj, short_taps, filters, grad_out, var_pos, alt_hidden):
    rows = hidden.shape[0]
    lanes = grad_out.shape[1]
    reach = filters.shape[1] + EDGE
    early = spread(filters), short_taps, var_pos
    if lax.axis_size("seq") == 8:
        feature, early = cube_features(hidden, alt_hidden, proj, early)
    else:
        feature = gathered_features((hidden, alt_hidden), proj, lanes)
    per_channel, short_taps, picks = early
    before = shifted(
        jnp.concatenate(
            [
                feature[1, rows - reach : rows],
                feature[2, rows - reach : rows],
                feature[0, rows - EDGE : rows],
            ],
            0,
        ),
        "seq",
        1,
    )
    after = shifted(
        jnp.concatenate(
            [
                feature[0, :reach],
                feature[1, :EDGE],
                feature[2, :EDGE],
                grad_out[:reach].astype(jnp.float32),
            ],
            0,
        ), "seq", -1
    )
    scores = mixer(
        picks, feature, before, after, grad_out, short_taps, per_channel
    )
    return tuple(lax.psum(tuple(scores), "grp"))


def solution(mesh):
    in_specs = (
        P(("rep", "seq"), "grp"),
        P(None, "seq", "grp"),
        P(None, None, "grp"),
        P("grp", None),
        P(("rep", "seq"), "grp"),
        P(("rep", "seq")),
        P(("rep", "seq"), "grp"),
    )
    out_specs = (P(("rep", "seq")), P(("rep", "seq")))
    return jax.shard_map(
        per_device, mesh=mesh, in_specs=in_specs, out_specs=out_specs, check_vma=False
    )
```

```python
import functools

import jax
import jax.numpy as jnp
from jax import lax
from jax.experimental import pallas as pl
from jax.experimental.pallas import tpu as pltpu
from jax.sharding import PartitionSpec as P

D = 8192
GROUP = 16
EDGE = 8
PIECES = 2
AXES = ("rep", "seq", "grp")
VMEM = pl.BlockSpec(memory_space=pltpu.VMEM)
ANY = pl.BlockSpec(memory_space=pl.ANY)
HBM = pl.BlockSpec(memory_space=pltpu.HBM)
SMEM = pl.BlockSpec(memory_space=pltpu.SMEM)


def paired(block, axis, first):
    route = []
    for left in range(first, lax.axis_size(axis) - 1, 2):
        route += [(left, left + 1), (left + 1, left)]
    return lax.ppermute(block, axis, route)


def crossed(block, axis, bit):
    return lax.ppermute(block, axis, [(i, i ^ bit) for i in range(lax.axis_size(axis))])


def moved(pairs, sems):
    copies = [
        pltpu.make_async_copy(source, target, sems.at[index])
        for index, (source, target) in enumerate(pairs)
    ]
    for copy in copies:
        copy.start()
    return copies


def part(side, width):
    return pl.ds(pl.multiple_of(side * width, width), width)


def panels_kernel(proj, own, first, second, sems):
    width = own.shape[2]
    cut = first.shape[1]
    home = part(lax.axis_index("rep"), width)
    copies = moved(
        [
            (proj.at[:, :, home], own),
            (proj.at[:, :cut, home], first),
            (proj.at[:, cut:, home], second),
        ],
        sems,
    )
    for copy in copies:
        copy.wait()


def panels(proj, width):
    kinds, height, _ = proj.shape
    shapes = [(kinds, height, width)] + [(kinds, height // 2, width)] * 2
    return pl.pallas_call(
        panels_kernel,
        out_shape=[jax.ShapeDtypeStruct(shape, proj.dtype) for shape in shapes],
        in_specs=[ANY],
        out_specs=[VMEM] * 3,
        scratch_shapes=[pltpu.SemaphoreType.DMA((3,))],
        compiler_params=pltpu.CompilerParams(vmem_limit_bytes=2 << 20),
        name="panels",
    )(proj)


def columns_kernel(tokens, alternates, theirs, sems):
    rows = tokens.shape[0]
    away = part(1 - lax.axis_index("rep"), theirs.shape[1])
    step = rows // PIECES
    copies = moved(
        [(alternates.at[:, away], theirs.at[rows:])]
        + [
            (tokens.at[begin : begin + step, away], theirs.at[begin : begin + step])
            for begin in range(0, rows, step)
        ],
        sems,
    )
    for copy in copies:
        copy.wait()


def columns(tokens, alternates, width):
    count = tokens.shape[0] + alternates.shape[0]
    return pl.pallas_call(
        columns_kernel,
        out_shape=jax.ShapeDtypeStruct((count, width), tokens.dtype),
        in_specs=[ANY] * 2,
        out_specs=VMEM,
        scratch_shapes=[pltpu.SemaphoreType.DMA((1 + PIECES,))],
        compiler_params=pltpu.CompilerParams(vmem_limit_bytes=3 << 20),
        name="columns",
    )(tokens, alternates)


def dots(tokens, panel, give, keep):
    kinds, _, lanes = give.shape
    size = kinds * lanes
    for begin, out in ((size, give), (0, keep)):
        result = lax.dot_general(
            tokens[...],
            panel[begin : begin + size],
            (((1,), (1,)), ((), ())),
            preferred_element_type=jnp.float32,
        )
        for kind in range(kinds):
            out[kind] = result[:, kind * lanes : (kind + 1) * lanes]


def theirs_kernel(theirs, *refs):
    blocks, (give, keep, panel) = refs[:-3], refs[-3:]
    kinds, _, lanes = give.shape
    quarter = lanes // 4
    seq = lax.axis_index("seq")
    swap = lax.axis_index("grp") ^ (seq // 4)
    done = 0
    for block in blocks:
        height = block.shape[1]
        order = done // quarter
        side = ((order // 4) ^ swap) * kinds * lanes
        at = ((seq % 4) ^ (order % 4)) * quarter + done % quarter
        for kind in range(kinds):
            panel[pl.ds(pl.multiple_of(side + kind * lanes + at, 16), height), :] = block[kind]
        done += height
    dots(theirs, panel, give, keep)


def ours_kernel(tokens, alternates, panel, give, keep, ours, sems):
    rows = tokens.shape[0]
    home = part(lax.axis_index("rep"), ours.shape[1])
    copies = moved(
        [(tokens.at[:, home], ours.at[:rows]), (alternates.at[:, home], ours.at[rows:])], sems
    )
    for copy in copies:
        copy.wait()
    dots(ours, panel, give, keep)


def products(tokens, alternates, theirs, blocks):
    count, width = theirs.shape
    kinds = blocks[0].shape[0]
    lanes = sum(block.shape[1] for block in blocks) // 2
    half = jax.ShapeDtypeStruct((kinds, count, lanes), jnp.float32)
    params = pltpu.CompilerParams(vmem_limit_bytes=10 << 20)
    cost = pl.CostEstimate(
        flops=4 * count * kinds * lanes * width,
        bytes_accessed=2 * width * (count + 2 * kinds * lanes) + 8 * kinds * count * lanes,
        transcendentals=0,
    )
    give_other, keep_other, panel = pl.pallas_call(
        theirs_kernel,
        out_shape=[half, half, jax.ShapeDtypeStruct((2 * kinds * lanes, width), theirs.dtype)],
        in_specs=[VMEM] * (1 + len(blocks)),
        out_specs=[VMEM] * 3,
        compiler_params=params,
        cost_estimate=cost,
        name="theirs",
    )(theirs, *blocks)
    give_mine, keep_mine = pl.pallas_call(
        ours_kernel,
        out_shape=[half, half],
        in_specs=[ANY, ANY, VMEM],
        out_specs=[VMEM] * 2,
        scratch_shapes=[pltpu.VMEM((count, width), theirs.dtype), pltpu.SemaphoreType.DMA((2,))],
        compiler_params=params,
        cost_estimate=cost,
        name="ours",
    )(tokens, alternates, panel)
    return give_other, keep_other, give_mine, keep_mine


def spread_kernel(filters, out):
    groups, lanes = filters.shape[0], out.shape[1]
    row = lax.broadcasted_iota(jnp.int32, (groups, lanes), 0)
    lane = lax.broadcasted_iota(jnp.int32, (groups, lanes), 1)
    out[...] = lax.dot_general(
        filters[...],
        jnp.where(lane // GROUP == row, 1.0, 0.0),
        (((0,), (0,)), ((), ())),
        precision=lax.Precision.HIGHEST,
        preferred_element_type=jnp.float32,
    )


def spread(filters):
    groups, span = filters.shape
    return pl.pallas_call(
        spread_kernel,
        out_shape=jax.ShapeDtypeStruct((span, groups * GROUP), jnp.float32),
        in_specs=[VMEM],
        out_specs=VMEM,
        compiler_params=pltpu.CompilerParams(vmem_limit_bytes=2 << 20),
        name="spread",
    )(filters)


def tap(taps, offset, index):
    return taps[offset, index : index + 1, :]


def mixed(taps, index, extended, begin, count):
    total = tap(taps, 0, index) * extended[begin : begin + count]
    for offset in (1, 2):
        total = total + tap(taps, offset, index) * extended[begin - offset : begin - offset + count]
    return total


def edges_kernel(span, rows, grad, taps, *refs):
    terms, (feature, within, across, before, after, head) = refs[:-6], refs[-6:]
    for kind in range(3):
        total = terms[0][kind]
        for term in terms[1:]:
            total = total + term[kind]
        feature[kind] = total
    begin = rows - span
    before[:span] = mixed(taps, 1, feature.at[1], begin, span) * mixed(
        taps, 2, feature.at[2], begin, span
    )
    for place, kind in enumerate((1, 2, 0)):
        at = span + place * EDGE
        before[at : at + EDGE] = feature[kind, rows - EDGE : rows]
    before[span + 3 * EDGE :] = jnp.zeros((2 * EDGE, head.shape[1]), jnp.float32)
    reach = span + EDGE
    head[:EDGE] = jnp.zeros((EDGE, head.shape[1]), jnp.float32)
    head[EDGE:] = feature[0, :reach]
    slope = grad[:reach].astype(jnp.float32)
    after[:reach] = slope * mixed(taps, 0, head, EDGE, reach)
    for kind in range(3):
        at = reach + kind * EDGE
        after[at : at + EDGE] = feature[kind, :EDGE]
    after[reach + 3 * EDGE :] = slope[:EDGE]
    even = lax.axis_index("seq") % 2 == 0
    within[...] = jnp.where(even, before[...], after[...])
    across[...] = jnp.where(even, after[...], before[...])


def edges(grad, taps, span, terms):
    rows, lanes = grad.shape
    size = span + 5 * EDGE
    return pl.pallas_call(
        functools.partial(edges_kernel, span, rows),
        out_shape=[jax.ShapeDtypeStruct(terms[0].shape, jnp.float32)]
        + [jax.ShapeDtypeStruct((size, lanes), jnp.float32)] * 2,
        in_specs=[VMEM] * (2 + len(terms)),
        out_specs=[VMEM] * 3,
        scratch_shapes=[pltpu.VMEM((size, lanes), jnp.float32)] * 2
        + [pltpu.VMEM((span + 2 * EDGE, lanes), jnp.float32)],
        compiler_params=pltpu.CompilerParams(vmem_limit_bytes=6 << 20),
        name="edges",
    )(grad, taps, *terms)


def mixer_kernel(
    rows, picks, feature, within, across, grad, taps, filters, out, effects,
    before, after, query, key, value, product, back_filtered, shifts, grads, summed,
):
    span, lanes = filters.shape
    variants = picks.shape[0]
    first = lax.axis_index("seq") * rows
    ahead = rows + EDGE
    reach = span + EDGE
    even = lax.axis_index("seq") % 2 == 0
    before[...] = jnp.where(even, across[...], within[...])
    after[...] = jnp.where(even, within[...], across[...])
    for kind, place, extended in ((1, 0, key), (2, 1, value), (0, 2, query)):
        extended[:EDGE] = before[span + place * EDGE : span + (place + 1) * EDGE]
        extended[EDGE:ahead] = feature[kind, :rows]
        extended[ahead:] = after[reach + kind * EDGE : reach + (kind + 1) * EDGE]
    slope_after = after[reach + 3 * EDGE :]
    key[EDGE:] = mixed(taps, 1, key, EDGE, ahead)
    value[EDGE:] = mixed(taps, 2, value, EDGE, ahead)
    product[:span] = before[:span]
    product[span:] = key[EDGE:] * value[EDGE:]
    query[EDGE:] = mixed(taps, 0, query, EDGE, ahead)
    back_filtered[:rows] = grad[...].astype(jnp.float32) * query[EDGE:ahead]
    back_filtered[rows:ahead] = slope_after * query[ahead:]
    back_filtered[ahead:] = after[EDGE:reach]

    def long_filter(source, later):
        length = source.shape[0]
        for shift in range(8):
            shifts[shift, : length - shift] = source[shift:]

        def accumulate(block, total):
            for inner in range(8):
                offset = block * 8 + inner
                if later:
                    shift, begin = inner, block
                else:
                    shift, begin = -inner % 8, span // 8 - block - (inner > 0)
                begin = pl.multiple_of(begin * 8, 8)
                total = total + filters[pl.ds(offset, 1), :] * shifts[shift, pl.ds(begin, ahead), :]
            return total

        return lax.fori_loop(0, span // 8, accumulate, jnp.zeros((ahead, lanes), jnp.float32))

    filtered = long_filter(product, False)
    grads[0, :rows] = grad[...].astype(jnp.float32) * filtered[:rows]
    grads[0, rows:] = slope_after * filtered[rows:]
    back_product = long_filter(back_filtered, True)
    grads[1] = back_product * value[EDGE:]
    grads[2] = back_product * key[EDGE:]
    total = jnp.zeros((rows, lanes), jnp.float32)
    for index in range(3):
        back = tap(taps, 0, index) * grads[index, :rows]
        for offset in (1, 2):
            back = back + tap(taps, offset, index) * grads[index, offset : offset + rows]
        back = back.astype(jnp.bfloat16).astype(jnp.float32)
        grads[index, :rows] = back
        total = total + back * feature[index, :rows]
    summed[:rows] = total
    for variant in range(variants):
        at = picks[variant] - first
        change = jnp.zeros((1, lanes), jnp.float32)
        for index in range(3):
            alternate = feature[index, rows + variant : rows + variant + 1]
            present = feature[index, pl.ds(at, 1)]
            change = change + grads[index, pl.ds(at, 1)] * (alternate - present)
        summed[rows + variant : rows + variant + 1] = change
    scores = lax.dot_general(
        jnp.full((8, lanes), 1.0, jnp.float32),
        summed[...],
        (((1,), (1,)), ((), ())),
        precision=lax.Precision.HIGHEST,
        preferred_element_type=jnp.float32,
    )
    scores = scores * D ** (-0.5)
    out[...] = scores[0, :rows]
    effects[...] = scores[0, rows:]


def mixer(picks, feature, within, across, grad, taps, filters):
    rows, lanes = grad.shape
    span = filters.shape[0]
    count = feature.shape[1]

    def body(*refs):
        mixer_kernel(rows, *refs)

    length = span + rows + EDGE
    return pl.pallas_call(
        body,
        out_shape=[
            jax.ShapeDtypeStruct((rows,), jnp.float32),
            jax.ShapeDtypeStruct((count - rows,), jnp.float32),
        ],
        in_specs=[SMEM] + [VMEM] * 6,
        out_specs=[VMEM, VMEM],
        scratch_shapes=[pltpu.VMEM((span + 5 * EDGE, lanes), jnp.float32)] * 2
        + [pltpu.VMEM((rows + 2 * EDGE, lanes), jnp.float32)] * 3
        + [
            pltpu.VMEM((length, lanes), jnp.float32),
            pltpu.VMEM((length, lanes), jnp.float32),
            pltpu.VMEM((8, length, lanes), jnp.float32),
            pltpu.VMEM((3, rows + EDGE, lanes), jnp.float32),
            pltpu.VMEM((count, lanes), jnp.float32),
        ],
        compiler_params=pltpu.CompilerParams(vmem_limit_bytes=8 << 20),
        name="mixer",
    )(picks, feature, within, across, grad, taps, filters)


def gathered_features(tokens, proj, lanes):
    rep, half = lax.axis_index("rep"), lax.axis_index("grp")
    width = proj.shape[2] // lax.axis_size("rep")
    count = sum(piece.shape[0] for piece in tokens)

    def columns(side):
        return jnp.concatenate(
            [lax.dynamic_slice_in_dim(piece, side * width, width, 1) for piece in tokens], 0
        )

    theirs = crossed(columns(1 - rep), "rep", 1)
    panels = lax.all_gather(
        lax.dynamic_slice_in_dim(proj, rep * width, width, 2), "seq", axis=1, tiled=True
    )
    both = jnp.concatenate([columns(rep), theirs], 0)
    partial = jnp.einsum("td,fcd->ftc", both, panels, preferred_element_type=jnp.float32)
    keep = lax.dynamic_slice_in_dim(partial, half * lanes, lanes, 2)
    give = lax.dynamic_slice_in_dim(partial, (1 - half) * lanes, lanes, 2)
    chip = keep + crossed(give, "grp", 1)
    return chip[:, :count], crossed(chip[:, count:], "rep", 1)


def cube_features(tokens, alternates, proj, early):
    width = proj.shape[2] // lax.axis_size("rep")
    bar = lax.optimization_barrier

    own, own_a, own_b = panels(proj, width)
    own_4a = crossed(own_a, "seq", 4)
    own_4b = crossed(own_b, "seq", 4)
    own_2 = crossed(own, "seq", 2)
    own_1 = crossed(own, "seq", 1)
    theirs = crossed(columns(tokens, alternates, width), "rep", 1)
    own_2, own_1, own_4a = bar((own_2, own_1, own_4a))
    own_3 = crossed(own_2, "seq", 1)
    own_4a, own_4b, own_3, early = bar((own_4a, own_4b, own_3, early))
    own_6a = crossed(own_4a, "seq", 2)
    own_6b = crossed(own_4b, "seq", 2)
    own_5b = crossed(own_4b, "seq", 1)
    own_5a = crossed(own_4a, "seq", 1)
    own_6a, own_6b, own_5a, own_5b = bar((own_6a, own_6b, own_5a, own_5b))
    own_7a = crossed(own_6a, "seq", 1)
    own_7b = crossed(own_5b, "seq", 2)

    near = own, own_1, own_2, own_3
    far = own_4a, own_4b, own_5a, own_5b, own_6a, own_6b, own_7a, own_7b
    give_other, keep_other, give_mine, keep_mine = products(tokens, alternates, theirs, near + far)
    other = crossed(keep_other + crossed(give_other, "grp", 1), "rep", 1)
    return (keep_mine, crossed(give_mine, "grp", 1), other), early


def per_device(hidden, proj, short_taps, filters, grad_out, var_pos, alt_hidden):
    lanes = grad_out.shape[1]
    early = spread(filters), short_taps, var_pos
    if lax.axis_size("seq") == 8:
        terms, early = cube_features(hidden, alt_hidden, proj, early)
    else:
        terms = gathered_features((hidden, alt_hidden), proj, lanes)
    per_channel, short_taps, picks = early
    feature, within, across = edges(grad_out, short_taps, filters.shape[1], terms)
    within, across = paired(within, "seq", 0), paired(across, "seq", 1)
    scores = mixer(picks, feature, within, across, grad_out, short_taps, per_channel)
    return tuple(lax.psum(tuple(scores), "grp"))


def solution(mesh):
    in_specs = (
        P(("rep", "seq"), "grp"),
        P(None, "seq", "grp"),
        P(None, None, "grp"),
        P("grp", None),
        P(("rep", "seq"), "grp"),
        P(("rep", "seq")),
        P(("rep", "seq"), "grp"),
    )
    out_specs = (P(("rep", "seq")), P(("rep", "seq")))
    return jax.shard_map(
        per_device, mesh=mesh, in_specs=in_specs, out_specs=out_specs, check_vma=False
    )
```

```python
import functools

import jax
import jax.numpy as jnp
from jax import lax
from jax.experimental import pallas as pl
from jax.experimental.pallas import tpu as pltpu
from jax.sharding import PartitionSpec as P

D = 8192
GROUP = 16
EDGE = 8
BAND = 96
PIECES = 2
AXES = ("rep", "seq", "grp")
VMEM = pl.BlockSpec(memory_space=pltpu.VMEM)
ANY = pl.BlockSpec(memory_space=pl.ANY)
HBM = pl.BlockSpec(memory_space=pltpu.HBM)
SMEM = pl.BlockSpec(memory_space=pltpu.SMEM)


def paired(block, axis, first):
    route = []
    for left in range(first, lax.axis_size(axis) - 1, 2):
        route += [(left, left + 1), (left + 1, left)]
    return lax.ppermute(block, axis, route)


def crossed(block, axis, bit):
    return lax.ppermute(block, axis, [(i, i ^ bit) for i in range(lax.axis_size(axis))])


def moved(pairs, sems):
    copies = [
        pltpu.make_async_copy(source, target, sems.at[index])
        for index, (source, target) in enumerate(pairs)
    ]
    for copy in copies:
        copy.start()
    return copies


def part(side, width):
    return pl.ds(pl.multiple_of(side * width, width), width)


def panels_kernel(proj, own, first, second, sems):
    width = own.shape[2]
    cut = first.shape[1]
    home = part(lax.axis_index("rep"), width)
    copies = moved(
        [
            (proj.at[:, :, home], own),
            (proj.at[:, :cut, home], first),
            (proj.at[:, cut:, home], second),
        ],
        sems,
    )
    for copy in copies:
        copy.wait()


def panels(proj, width):
    kinds, height, _ = proj.shape
    shapes = [(kinds, height, width)] + [(kinds, height // 2, width)] * 2
    return pl.pallas_call(
        panels_kernel,
        out_shape=[jax.ShapeDtypeStruct(shape, proj.dtype) for shape in shapes],
        in_specs=[ANY],
        out_specs=[VMEM] * 3,
        scratch_shapes=[pltpu.SemaphoreType.DMA((3,))],
        compiler_params=pltpu.CompilerParams(vmem_limit_bytes=2 << 20),
        name="panels",
    )(proj)


def columns_kernel(tokens, alternates, theirs, sems):
    rows = tokens.shape[0]
    away = part(1 - lax.axis_index("rep"), theirs.shape[1])
    step = rows // PIECES
    copies = moved(
        [(alternates.at[:, away], theirs.at[rows:])]
        + [
            (tokens.at[begin : begin + step, away], theirs.at[begin : begin + step])
            for begin in range(0, rows, step)
        ],
        sems,
    )
    for copy in copies:
        copy.wait()


def columns(tokens, alternates, width):
    count = tokens.shape[0] + alternates.shape[0]
    return pl.pallas_call(
        columns_kernel,
        out_shape=jax.ShapeDtypeStruct((count, width), tokens.dtype),
        in_specs=[ANY] * 2,
        out_specs=VMEM,
        scratch_shapes=[pltpu.SemaphoreType.DMA((1 + PIECES,))],
        compiler_params=pltpu.CompilerParams(vmem_limit_bytes=3 << 20),
        name="columns",
    )(tokens, alternates)


def dots(tokens, panel, give, keep):
    kinds, _, lanes = keep.shape
    size = kinds * lanes
    for begin, out in ((size, give), (0, keep)):
        result = lax.dot_general(
            tokens[...],
            panel[begin : begin + size],
            (((1,), (1,)), ((), ())),
            preferred_element_type=jnp.float32,
        )
        for kind in range(kinds):
            out_part = out[kind] if isinstance(out, tuple) else out.at[kind]
            out_part[...] = result[:, kind * lanes : (kind + 1) * lanes]


def theirs_kernel(theirs, *refs):
    blocks, (give, keep, panel) = refs[:-3], refs[-3:]
    kinds, _, lanes = give.shape
    quarter = lanes // 4
    seq = lax.axis_index("seq")
    swap = lax.axis_index("grp") ^ (seq // 4)
    done = 0
    for block in blocks:
        height = block.shape[1]
        order = done // quarter
        side = ((order // 4) ^ swap) * kinds * lanes
        at = ((seq % 4) ^ (order % 4)) * quarter + done % quarter
        for kind in range(kinds):
            panel[pl.ds(pl.multiple_of(side + kind * lanes + at, 16), height), :] = block[kind]
        done += height
    dots(theirs, panel, give, keep)


def ours_kernel(tokens, alternates, panel, give_query, give_key, give_value, keep, ours, sems):
    rows = tokens.shape[0]
    home = part(lax.axis_index("rep"), ours.shape[1])
    copies = moved(
        [(tokens.at[:, home], ours.at[:rows]), (alternates.at[:, home], ours.at[rows:])], sems
    )
    for copy in copies:
        copy.wait()
    dots(ours, panel, (give_query, give_key, give_value), keep)


def products(tokens, alternates, theirs, blocks):
    count, width = theirs.shape
    kinds = blocks[0].shape[0]
    lanes = sum(block.shape[1] for block in blocks) // 2
    half = jax.ShapeDtypeStruct((kinds, count, lanes), jnp.float32)
    params = pltpu.CompilerParams(vmem_limit_bytes=10 << 20)
    cost = pl.CostEstimate(
        flops=4 * count * kinds * lanes * width,
        bytes_accessed=2 * width * (count + 2 * kinds * lanes) + 8 * kinds * count * lanes,
        transcendentals=0,
    )
    give_other, keep_other, panel = pl.pallas_call(
        theirs_kernel,
        out_shape=[half, half, jax.ShapeDtypeStruct((2 * kinds * lanes, width), theirs.dtype)],
        in_specs=[VMEM] * (1 + len(blocks)),
        out_specs=[VMEM] * 3,
        compiler_params=params,
        cost_estimate=cost,
        name="theirs",
    )(theirs, *blocks)
    *give_mine, keep_mine = pl.pallas_call(
        ours_kernel,
        out_shape=[jax.ShapeDtypeStruct((count, lanes), jnp.float32)] * kinds + [half],
        in_specs=[ANY, ANY, VMEM],
        out_specs=[VMEM] * (kinds + 1),
        scratch_shapes=[pltpu.VMEM((count, width), theirs.dtype), pltpu.SemaphoreType.DMA((2,))],
        compiler_params=params,
        cost_estimate=cost,
        name="ours",
    )(tokens, alternates, panel)
    return give_other, keep_other, give_mine, keep_mine


def bands_kernel(filters, *outs):
    groups, span = filters.shape
    deep = 2 * span
    row = lax.broadcasted_iota(jnp.int32, (span, deep), 0)
    column = lax.broadcasted_iota(jnp.int32, (span, deep), 1)
    for later in (False, True):
        place = jnp.where(column == (row if later else span - row), 1.0, 0.0)
        taps = lax.dot_general(
            filters[...],
            place,
            (((1,), (0,)), ((), ())),
            precision=lax.Precision.HIGHEST,
            preferred_element_type=jnp.float32,
        )
        for group in range(groups):
            band = jnp.broadcast_to(taps[group : group + 1], (BAND, deep))
            band = pltpu.roll(band, 0, 1, stride=1, stride_axis=0)
            high = band.astype(jnp.bfloat16)
            at = pl.ds(group * BAND, BAND)
            outs[2 * later][at] = high
            outs[2 * later + 1][at] = (band - high.astype(jnp.float32)).astype(jnp.bfloat16)


def bands(filters):
    groups, span = filters.shape
    return pl.pallas_call(
        bands_kernel,
        out_shape=[jax.ShapeDtypeStruct((groups * BAND, 2 * span), jnp.bfloat16)] * 4,
        in_specs=[VMEM],
        out_specs=[VMEM] * 4,
        compiler_params=pltpu.CompilerParams(vmem_limit_bytes=4 << 20),
        name="bands",
    )(filters)


def tap(taps, offset, index):
    return taps[offset, index : index + 1, :]


def mixed(taps, index, extended, begin, count):
    total = tap(taps, 0, index) * extended[begin : begin + count]
    for offset in (1, 2):
        total = total + tap(taps, offset, index) * extended[begin - offset : begin - offset + count]
    return total


def edges_kernel(span, rows, grad, taps, *refs):
    terms, (feature, within, across, before, after, head) = refs[:-6], refs[-6:]
    for kind in range(3):
        total = terms[0][kind] + terms[1][kind]
        if len(terms) > 2:
            total = total + terms[2 + kind][...]
        feature[kind] = total
    begin = rows - span
    before[:span] = mixed(taps, 1, feature.at[1], begin, span) * mixed(
        taps, 2, feature.at[2], begin, span
    )
    for place, kind in enumerate((1, 2, 0)):
        at = span + place * EDGE
        before[at : at + EDGE] = feature[kind, rows - EDGE : rows]
    before[span + 3 * EDGE :] = jnp.zeros((2 * EDGE, head.shape[1]), jnp.float32)
    reach = span + EDGE
    head[:EDGE] = jnp.zeros((EDGE, head.shape[1]), jnp.float32)
    head[EDGE:] = feature[0, :reach]
    slope = grad[:reach].astype(jnp.float32)
    after[:reach] = slope * mixed(taps, 0, head, EDGE, reach)
    for kind in range(3):
        at = reach + kind * EDGE
        after[at : at + EDGE] = feature[kind, :EDGE]
    after[reach + 3 * EDGE :] = slope[:EDGE]
    even = lax.axis_index("seq") % 2 == 0
    within[...] = jnp.where(even, before[...], after[...])
    across[...] = jnp.where(even, after[...], before[...])


def edges(grad, taps, span, terms):
    rows, lanes = grad.shape
    size = span + 5 * EDGE
    return pl.pallas_call(
        functools.partial(edges_kernel, span, rows),
        out_shape=[jax.ShapeDtypeStruct(terms[0].shape, jnp.float32)]
        + [jax.ShapeDtypeStruct((size, lanes), jnp.float32)] * 2,
        in_specs=[VMEM] * (2 + len(terms)),
        out_specs=[VMEM] * 3,
        scratch_shapes=[pltpu.VMEM((size, lanes), jnp.float32)] * 2
        + [pltpu.VMEM((span + 2 * EDGE, lanes), jnp.float32)],
        compiler_params=pltpu.CompilerParams(vmem_limit_bytes=6 << 20),
        name="edges",
    )(grad, taps, *terms)


def mixer_kernel(
    rows, span, picks, feature, within, across, grad, taps, high, low, later_high, later_low,
    out, effects, before, after, query, key, value, product, back_filtered, filtered,
    back_product, grads, summed,
):
    lanes = grad.shape[1]
    variants = picks.shape[0]
    first = lax.axis_index("seq") * rows
    ahead = rows + EDGE
    reach = span + EDGE
    even = lax.axis_index("seq") % 2 == 0
    before[...] = jnp.where(even, across[...], within[...])
    after[...] = jnp.where(even, within[...], across[...])
    for kind, place, extended in ((1, 0, key), (2, 1, value), (0, 2, query)):
        extended[:EDGE] = before[span + place * EDGE : span + (place + 1) * EDGE]
        extended[EDGE:ahead] = feature[kind, :rows]
        extended[ahead:] = after[reach + kind * EDGE : reach + (kind + 1) * EDGE]
    slope_after = after[reach + 3 * EDGE :]
    key[EDGE:] = mixed(taps, 1, key, EDGE, ahead)
    value[EDGE:] = mixed(taps, 2, value, EDGE, ahead)
    product[:span] = before[:span]
    product[span : span + ahead] = key[EDGE:] * value[EDGE:]
    product[span + ahead :] = jnp.zeros((product.shape[0] - span - ahead, lanes), jnp.float32)
    query[EDGE:] = mixed(taps, 0, query, EDGE, ahead)
    back_filtered[:rows] = grad[...].astype(jnp.float32) * query[EDGE:ahead]
    back_filtered[rows:ahead] = slope_after * query[ahead:]
    back_filtered[ahead : rows + reach] = after[EDGE:reach]
    back_filtered[rows + reach :] = jnp.zeros(
        (back_filtered.shape[0] - rows - reach, lanes), jnp.float32
    )

    owner = lax.broadcasted_iota(jnp.int32, (BAND, lanes), 1) // GROUP

    def long_filter(source, high, low, out):
        for begin in range(0, out.shape[0], BAND):
            section = source[begin : begin + 2 * span]
            upper = section.astype(jnp.bfloat16)
            lower = (section - upper.astype(jnp.float32)).astype(jnp.bfloat16)
            both = jnp.dot(
                high[...], jnp.concatenate([upper, lower], 1), preferred_element_type=jnp.float32
            )
            rest = jnp.dot(low[...], upper, preferred_element_type=jnp.float32)
            summed = both[:, :lanes] + both[:, lanes:] + rest
            chosen = summed[:BAND]
            for group in range(1, lanes // GROUP):
                chosen = jnp.where(
                    owner == group, summed[group * BAND : (group + 1) * BAND], chosen
                )
            out[begin : begin + BAND] = chosen

    long_filter(product, high, low, filtered)
    long_filter(back_filtered, later_high, later_low, back_product)
    grads[0, :rows] = grad[...].astype(jnp.float32) * filtered[:rows]
    grads[0, rows:] = slope_after * filtered[rows:ahead]
    grads[1] = back_product[:ahead] * value[EDGE:]
    grads[2] = back_product[:ahead] * key[EDGE:]
    total = jnp.zeros((rows, lanes), jnp.float32)
    for index in range(3):
        back = tap(taps, 0, index) * grads[index, :rows]
        for offset in (1, 2):
            back = back + tap(taps, offset, index) * grads[index, offset : offset + rows]
        back = back.astype(jnp.bfloat16).astype(jnp.float32)
        grads[index, :rows] = back
        total = total + back * feature[index, :rows]
    summed[:rows] = total
    for variant in range(variants):
        at = picks[variant] - first
        change = jnp.zeros((1, lanes), jnp.float32)
        for index in range(3):
            alternate = feature[index, rows + variant : rows + variant + 1]
            present = feature[index, pl.ds(at, 1)]
            change = change + grads[index, pl.ds(at, 1)] * (alternate - present)
        summed[rows + variant : rows + variant + 1] = change
    scores = lax.dot_general(
        jnp.full((8, lanes), 1.0, jnp.float32),
        summed[...],
        (((1,), (1,)), ((), ())),
        precision=lax.Precision.HIGHEST,
        preferred_element_type=jnp.float32,
    )
    scores = scores * D ** (-0.5)
    out[...] = scores[0, :rows]
    effects[...] = scores[0, rows:]


def mixer(picks, feature, within, across, grad, taps, span, weights):
    rows, lanes = grad.shape
    count = feature.shape[1]

    def body(*refs):
        mixer_kernel(rows, span, *refs)

    steps = pl.cdiv(rows + EDGE, BAND)
    length = (steps - 1) * BAND + 2 * span
    return pl.pallas_call(
        body,
        out_shape=[
            jax.ShapeDtypeStruct((rows,), jnp.float32),
            jax.ShapeDtypeStruct((count - rows,), jnp.float32),
        ],
        in_specs=[SMEM] + [VMEM] * 9,
        out_specs=[VMEM, VMEM],
        scratch_shapes=[pltpu.VMEM((span + 5 * EDGE, lanes), jnp.float32)] * 2
        + [pltpu.VMEM((rows + 2 * EDGE, lanes), jnp.float32)] * 3
        + [
            pltpu.VMEM((length, lanes), jnp.float32),
            pltpu.VMEM((length, lanes), jnp.float32),
            pltpu.VMEM((steps * BAND, lanes), jnp.float32),
            pltpu.VMEM((steps * BAND, lanes), jnp.float32),
            pltpu.VMEM((3, rows + EDGE, lanes), jnp.float32),
            pltpu.VMEM((count, lanes), jnp.float32),
        ],
        compiler_params=pltpu.CompilerParams(vmem_limit_bytes=12 << 20),
        name="mixer",
    )(picks, feature, within, across, grad, taps, *weights)


def gathered_features(tokens, proj, lanes):
    rep, half = lax.axis_index("rep"), lax.axis_index("grp")
    width = proj.shape[2] // lax.axis_size("rep")
    count = sum(piece.shape[0] for piece in tokens)

    def columns(side):
        return jnp.concatenate(
            [lax.dynamic_slice_in_dim(piece, side * width, width, 1) for piece in tokens], 0
        )

    theirs = crossed(columns(1 - rep), "rep", 1)
    panels = lax.all_gather(
        lax.dynamic_slice_in_dim(proj, rep * width, width, 2), "seq", axis=1, tiled=True
    )
    both = jnp.concatenate([columns(rep), theirs], 0)
    partial = jnp.einsum("td,fcd->ftc", both, panels, preferred_element_type=jnp.float32)
    keep = lax.dynamic_slice_in_dim(partial, half * lanes, lanes, 2)
    give = lax.dynamic_slice_in_dim(partial, (1 - half) * lanes, lanes, 2)
    chip = keep + crossed(give, "grp", 1)
    return chip[:, :count], crossed(chip[:, count:], "rep", 1)


def cube_features(tokens, alternates, proj, early):
    width = proj.shape[2] // lax.axis_size("rep")
    bar = lax.optimization_barrier

    own, own_a, own_b = panels(proj, width)
    own_4a = crossed(own_a, "seq", 4)
    own_4b = crossed(own_b, "seq", 4)
    own_2 = crossed(own, "seq", 2)
    own_1 = crossed(own, "seq", 1)
    theirs = crossed(columns(tokens, alternates, width), "rep", 1)
    own_2, own_1, own_4a = bar((own_2, own_1, own_4a))
    own_3 = crossed(own_2, "seq", 1)
    own_4a, own_4b, own_3, early = bar((own_4a, own_4b, own_3, early))
    own_6a = crossed(own_4a, "seq", 2)
    own_6b = crossed(own_4b, "seq", 2)
    own_5b = crossed(own_4b, "seq", 1)
    own_5a = crossed(own_4a, "seq", 1)
    own_6a, own_6b, own_5a, own_5b = bar((own_6a, own_6b, own_5a, own_5b))
    own_7a = crossed(own_6a, "seq", 1)
    own_7b = crossed(own_5b, "seq", 2)

    near = own, own_1, own_2, own_3
    far = own_4a, own_4b, own_5a, own_5b, own_6a, own_6b, own_7a, own_7b
    give_other, keep_other, give_mine, keep_mine = products(tokens, alternates, theirs, near + far)
    other = crossed(keep_other + crossed(give_other, "grp", 1), "rep", 1)
    return (keep_mine, other) + tuple(crossed(part, "grp", 1) for part in give_mine), early


def per_device(hidden, proj, short_taps, filters, grad_out, var_pos, alt_hidden):
    lanes = grad_out.shape[1]
    span = filters.shape[1]
    early = bands(filters), short_taps, var_pos
    if lax.axis_size("seq") == 8:
        terms, early = cube_features(hidden, alt_hidden, proj, early)
    else:
        terms = gathered_features((hidden, alt_hidden), proj, lanes)
    weights, short_taps, picks = early
    feature, within, across = edges(grad_out, short_taps, span, terms)
    within, across = paired(within, "seq", 0), paired(across, "seq", 1)
    scores = mixer(picks, feature, within, across, grad_out, short_taps, span, weights)
    return tuple(lax.psum(tuple(scores), "grp"))


def solution(mesh):
    in_specs = (
        P(("rep", "seq"), "grp"),
        P(None, "seq", "grp"),
        P(None, None, "grp"),
        P("grp", None),
        P(("rep", "seq"), "grp"),
        P(("rep", "seq")),
        P(("rep", "seq"), "grp"),
    )
    out_specs = (P(("rep", "seq")), P(("rep", "seq")))
    return jax.shard_map(
        per_device, mesh=mesh, in_specs=in_specs, out_specs=out_specs, check_vma=False
    )
```

```python
import functools

import jax
import jax.numpy as jnp
from jax import lax
from jax.experimental import pallas as pl
from jax.experimental.pallas import tpu as pltpu
from jax.sharding import PartitionSpec as P

D = 8192
GROUP = 16
EDGE = 8
BAND = 96
PIECES = 2
AXES = ("rep", "seq", "grp")
VMEM = pl.BlockSpec(memory_space=pltpu.VMEM)
ANY = pl.BlockSpec(memory_space=pl.ANY)
HBM = pl.BlockSpec(memory_space=pltpu.HBM)
SMEM = pl.BlockSpec(memory_space=pltpu.SMEM)


def paired(block, axis, first):
    route = []
    for left in range(first, lax.axis_size(axis) - 1, 2):
        route += [(left, left + 1), (left + 1, left)]
    return lax.ppermute(block, axis, route)


def crossed(block, axis, bit):
    return lax.ppermute(block, axis, [(i, i ^ bit) for i in range(lax.axis_size(axis))])


def moved(pairs, sems):
    copies = [
        pltpu.make_async_copy(source, target, sems.at[index])
        for index, (source, target) in enumerate(pairs)
    ]
    for copy in copies:
        copy.start()
    return copies


def part(side, width):
    return pl.ds(pl.multiple_of(side * width, width), width)


def panels_kernel(proj, own, first, second, sems):
    width = own.shape[2]
    cut = first.shape[1]
    home = part(lax.axis_index("rep"), width)
    copies = moved(
        [
            (proj.at[:, :, home], own),
            (proj.at[:, :cut, home], first),
            (proj.at[:, cut:, home], second),
        ],
        sems,
    )
    for copy in copies:
        copy.wait()


def panels(proj, width):
    kinds, height, _ = proj.shape
    shapes = [(kinds, height, width)] + [(kinds, height // 2, width)] * 2
    return pl.pallas_call(
        panels_kernel,
        out_shape=[jax.ShapeDtypeStruct(shape, proj.dtype) for shape in shapes],
        in_specs=[ANY],
        out_specs=[VMEM] * 3,
        scratch_shapes=[pltpu.SemaphoreType.DMA((3,))],
        compiler_params=pltpu.CompilerParams(vmem_limit_bytes=2 << 20),
        name="panels",
    )(proj)


def columns_kernel(tokens, alternates, theirs, sems):
    rows = tokens.shape[0]
    away = part(1 - lax.axis_index("rep"), theirs.shape[1])
    step = rows // PIECES
    copies = moved(
        [(alternates.at[:, away], theirs.at[rows:])]
        + [
            (tokens.at[begin : begin + step, away], theirs.at[begin : begin + step])
            for begin in range(0, rows, step)
        ],
        sems,
    )
    for copy in copies:
        copy.wait()


def columns(tokens, alternates, width):
    count = tokens.shape[0] + alternates.shape[0]
    return pl.pallas_call(
        columns_kernel,
        out_shape=jax.ShapeDtypeStruct((count, width), tokens.dtype),
        in_specs=[ANY] * 2,
        out_specs=VMEM,
        scratch_shapes=[pltpu.SemaphoreType.DMA((1 + PIECES,))],
        compiler_params=pltpu.CompilerParams(vmem_limit_bytes=3 << 20),
        name="columns",
    )(tokens, alternates)


def dots(tokens, panel, side, outs):
    lanes = outs[0].shape[1]
    size = len(outs) * lanes
    result = lax.dot_general(
        tokens[...],
        panel[side * size : (side + 1) * size],
        (((1,), (1,)), ((), ())),
        preferred_element_type=jnp.float32,
    )
    for kind, out in enumerate(outs):
        out[...] = result[:, kind * lanes : (kind + 1) * lanes]


def kinds_of(out):
    return [out.at[kind] for kind in range(out.shape[0])]


def theirs_kernel(theirs, *refs):
    blocks, (give, panel) = refs[:-2], refs[-2:]
    kinds, _, lanes = give.shape
    quarter = lanes // 4
    seq = lax.axis_index("seq")
    swap = lax.axis_index("grp") ^ (seq // 4)
    done = 0
    for block in blocks:
        height = block.shape[1]
        order = done // quarter
        side = ((order // 4) ^ swap) * kinds * lanes
        at = ((seq % 4) ^ (order % 4)) * quarter + done % quarter
        for kind in range(kinds):
            panel[pl.ds(pl.multiple_of(side + kind * lanes + at, 16), height), :] = block[kind]
        done += height
    dots(theirs, panel, 1, kinds_of(give))


def keep_kernel(theirs, panel, keep):
    dots(theirs, panel, 0, kinds_of(keep))


def ours_kernel(tokens, alternates, panel, give_query, give_key, give_value, keep, ours, sems):
    rows = tokens.shape[0]
    home = part(lax.axis_index("rep"), ours.shape[1])
    copies = moved(
        [(tokens.at[:, home], ours.at[:rows]), (alternates.at[:, home], ours.at[rows:])], sems
    )
    for copy in copies:
        copy.wait()
    dots(ours, panel, 1, (give_query, give_key, give_value))
    dots(ours, panel, 0, kinds_of(keep))


def products(tokens, alternates, theirs, blocks):
    count, width = theirs.shape
    kinds = blocks[0].shape[0]
    lanes = sum(block.shape[1] for block in blocks) // 2
    half = jax.ShapeDtypeStruct((kinds, count, lanes), jnp.float32)
    params = pltpu.CompilerParams(vmem_limit_bytes=10 << 20)
    cost = pl.CostEstimate(
        flops=4 * count * kinds * lanes * width,
        bytes_accessed=2 * width * (count + 2 * kinds * lanes) + 8 * kinds * count * lanes,
        transcendentals=0,
    )
    give_other, panel = pl.pallas_call(
        theirs_kernel,
        out_shape=[half, jax.ShapeDtypeStruct((2 * kinds * lanes, width), theirs.dtype)],
        in_specs=[VMEM] * (1 + len(blocks)),
        out_specs=[VMEM] * 2,
        compiler_params=params,
        cost_estimate=cost,
        name="theirs",
    )(theirs, *blocks)
    keep_other = pl.pallas_call(
        keep_kernel,
        out_shape=half,
        in_specs=[VMEM] * 2,
        out_specs=VMEM,
        compiler_params=params,
        cost_estimate=cost,
        name="keep",
    )(theirs, panel)
    *give_mine, keep_mine = pl.pallas_call(
        ours_kernel,
        out_shape=[jax.ShapeDtypeStruct((count, lanes), jnp.float32)] * kinds + [half],
        in_specs=[ANY, ANY, VMEM],
        out_specs=[VMEM] * (kinds + 1),
        scratch_shapes=[pltpu.VMEM((count, width), theirs.dtype), pltpu.SemaphoreType.DMA((2,))],
        compiler_params=params,
        cost_estimate=cost,
        name="ours",
    )(tokens, alternates, panel)
    return give_other, keep_other, give_mine, keep_mine


def bands_kernel(filters, *outs):
    groups, span = filters.shape
    deep = 2 * span
    row = lax.broadcasted_iota(jnp.int32, (span, deep), 0)
    column = lax.broadcasted_iota(jnp.int32, (span, deep), 1)
    for later in (False, True):
        place = jnp.where(column == (row if later else span - row), 1.0, 0.0)
        taps = lax.dot_general(
            filters[...],
            place,
            (((1,), (0,)), ((), ())),
            precision=lax.Precision.HIGHEST,
            preferred_element_type=jnp.float32,
        )
        for group in range(groups):
            band = jnp.broadcast_to(taps[group : group + 1], (BAND, deep))
            band = pltpu.roll(band, 0, 1, stride=1, stride_axis=0)
            high = band.astype(jnp.bfloat16)
            at = pl.ds(group * BAND, BAND)
            outs[2 * later][at] = high
            outs[2 * later + 1][at] = (band - high.astype(jnp.float32)).astype(jnp.bfloat16)


def bands(filters):
    groups, span = filters.shape
    return pl.pallas_call(
        bands_kernel,
        out_shape=[jax.ShapeDtypeStruct((groups * BAND, 2 * span), jnp.bfloat16)] * 4,
        in_specs=[VMEM],
        out_specs=[VMEM] * 4,
        compiler_params=pltpu.CompilerParams(vmem_limit_bytes=4 << 20),
        name="bands",
    )(filters)


def tap(taps, offset, index):
    return taps[offset, index : index + 1, :]


def mixed(taps, index, extended, begin, count):
    total = tap(taps, 0, index) * extended[begin : begin + count]
    for offset in (1, 2):
        total = total + tap(taps, offset, index) * extended[begin - offset : begin - offset + count]
    return total


def edges_kernel(span, rows, grad, taps, *refs):
    terms, (feature, within, across, before, after, head) = refs[:-6], refs[-6:]
    for kind in range(3):
        total = terms[0][kind] + terms[1][kind]
        if len(terms) > 2:
            total = total + terms[2 + kind][...]
        feature[kind] = total
    begin = rows - span
    before[:span] = mixed(taps, 1, feature.at[1], begin, span) * mixed(
        taps, 2, feature.at[2], begin, span
    )
    for place, kind in enumerate((1, 2, 0)):
        at = span + place * EDGE
        before[at : at + EDGE] = feature[kind, rows - EDGE : rows]
    before[span + 3 * EDGE :] = jnp.zeros((2 * EDGE, head.shape[1]), jnp.float32)
    reach = span + EDGE
    head[:EDGE] = jnp.zeros((EDGE, head.shape[1]), jnp.float32)
    head[EDGE:] = feature[0, :reach]
    slope = grad[:reach].astype(jnp.float32)
    after[:reach] = slope * mixed(taps, 0, head, EDGE, reach)
    for kind in range(3):
        at = reach + kind * EDGE
        after[at : at + EDGE] = feature[kind, :EDGE]
    after[reach + 3 * EDGE :] = slope[:EDGE]
    even = lax.axis_index("seq") % 2 == 0
    within[...] = jnp.where(even, before[...], after[...])
    across[...] = jnp.where(even, after[...], before[...])


def edges(grad, taps, span, terms):
    rows, lanes = grad.shape
    size = span + 5 * EDGE
    return pl.pallas_call(
        functools.partial(edges_kernel, span, rows),
        out_shape=[jax.ShapeDtypeStruct(terms[0].shape, jnp.float32)]
        + [jax.ShapeDtypeStruct((size, lanes), jnp.float32)] * 2,
        in_specs=[VMEM] * (2 + len(terms)),
        out_specs=[VMEM] * 3,
        scratch_shapes=[pltpu.VMEM((size, lanes), jnp.float32)] * 2
        + [pltpu.VMEM((span + 2 * EDGE, lanes), jnp.float32)],
        compiler_params=pltpu.CompilerParams(vmem_limit_bytes=6 << 20),
        name="edges",
    )(grad, taps, *terms)


def mixer_kernel(
    rows, span, picks, feature, within, across, grad, taps, high, low, later_high, later_low,
    out, before, after, query, key, value, product, back_filtered, filtered,
    back_product, grads, summed,
):
    lanes = grad.shape[1]
    variants = picks.shape[0]
    first = lax.axis_index("seq") * rows
    ahead = rows + EDGE
    reach = span + EDGE
    even = lax.axis_index("seq") % 2 == 0
    before[...] = jnp.where(even, across[...], within[...])
    after[...] = jnp.where(even, within[...], across[...])
    for kind, place, extended in ((1, 0, key), (2, 1, value), (0, 2, query)):
        extended[:EDGE] = before[span + place * EDGE : span + (place + 1) * EDGE]
        extended[EDGE:ahead] = feature[kind, :rows]
        extended[ahead:] = after[reach + kind * EDGE : reach + (kind + 1) * EDGE]
    slope_after = after[reach + 3 * EDGE :]
    key[EDGE:] = mixed(taps, 1, key, EDGE, ahead)
    value[EDGE:] = mixed(taps, 2, value, EDGE, ahead)
    product[:span] = before[:span]
    product[span : span + ahead] = key[EDGE:] * value[EDGE:]
    product[span + ahead :] = jnp.zeros((product.shape[0] - span - ahead, lanes), jnp.float32)
    query[EDGE:] = mixed(taps, 0, query, EDGE, ahead)
    back_filtered[:rows] = grad[...].astype(jnp.float32) * query[EDGE:ahead]
    back_filtered[rows:ahead] = slope_after * query[ahead:]
    back_filtered[ahead : rows + reach] = after[EDGE:reach]
    back_filtered[rows + reach :] = jnp.zeros(
        (back_filtered.shape[0] - rows - reach, lanes), jnp.float32
    )

    owner = lax.broadcasted_iota(jnp.int32, (BAND, lanes), 1) // GROUP

    def long_filter(source, high, low, out):
        for begin in range(0, out.shape[0], BAND):
            section = source[begin : begin + 2 * span]
            upper = section.astype(jnp.bfloat16)
            lower = (section - upper.astype(jnp.float32)).astype(jnp.bfloat16)
            both = jnp.dot(
                high[...], jnp.concatenate([upper, lower], 1), preferred_element_type=jnp.float32
            )
            rest = jnp.dot(low[...], upper, preferred_element_type=jnp.float32)
            summed = both[:, :lanes] + both[:, lanes:] + rest
            chosen = summed[:BAND]
            for group in range(1, lanes // GROUP):
                chosen = jnp.where(
                    owner == group, summed[group * BAND : (group + 1) * BAND], chosen
                )
            out[begin : begin + BAND] = chosen

    long_filter(product, high, low, filtered)
    long_filter(back_filtered, later_high, later_low, back_product)
    grads[0, :rows] = grad[...].astype(jnp.float32) * filtered[:rows]
    grads[0, rows:] = slope_after * filtered[rows:ahead]
    grads[1] = back_product[:ahead] * value[EDGE:]
    grads[2] = back_product[:ahead] * key[EDGE:]
    total = jnp.zeros((rows, lanes), jnp.float32)
    for index in range(3):
        back = tap(taps, 0, index) * grads[index, :rows]
        for offset in (1, 2):
            back = back + tap(taps, offset, index) * grads[index, offset : offset + rows]
        back = back.astype(jnp.bfloat16).astype(jnp.float32)
        grads[index, :rows] = back
        total = total + back * feature[index, :rows]
    summed[:rows] = total
    for variant in range(variants):
        at = picks[variant] - first
        change = jnp.zeros((1, lanes), jnp.float32)
        for index in range(3):
            alternate = feature[index, rows + variant : rows + variant + 1]
            present = feature[index, pl.ds(at, 1)]
            change = change + grads[index, pl.ds(at, 1)] * (alternate - present)
        summed[rows + variant : rows + variant + 1] = change
    scores = lax.dot_general(
        jnp.full((8, lanes), 1.0, jnp.float32),
        summed[...],
        (((1,), (1,)), ((), ())),
        precision=lax.Precision.HIGHEST,
        preferred_element_type=jnp.float32,
    )
    out[...] = scores * D ** (-0.5)


def mixer(picks, feature, within, across, grad, taps, span, weights):
    rows, lanes = grad.shape
    count = feature.shape[1]

    def body(*refs):
        mixer_kernel(rows, span, *refs)

    steps = pl.cdiv(rows + EDGE, BAND)
    length = (steps - 1) * BAND + 2 * span
    return pl.pallas_call(
        body,
        out_shape=jax.ShapeDtypeStruct((8, count), jnp.float32),
        in_specs=[SMEM] + [VMEM] * 9,
        out_specs=VMEM,
        scratch_shapes=[pltpu.VMEM((span + 5 * EDGE, lanes), jnp.float32)] * 2
        + [pltpu.VMEM((rows + 2 * EDGE, lanes), jnp.float32)] * 3
        + [
            pltpu.VMEM((length, lanes), jnp.float32),
            pltpu.VMEM((length, lanes), jnp.float32),
            pltpu.VMEM((steps * BAND, lanes), jnp.float32),
            pltpu.VMEM((steps * BAND, lanes), jnp.float32),
            pltpu.VMEM((3, rows + EDGE, lanes), jnp.float32),
            pltpu.VMEM((count, lanes), jnp.float32),
        ],
        compiler_params=pltpu.CompilerParams(vmem_limit_bytes=12 << 20),
        name="mixer",
    )(picks, feature, within, across, grad, taps, *weights)


def total_kernel(mine, other, out, effects):
    rows = out.shape[0]
    scores = mine[:1] + other[:1]
    out[...] = scores[0, :rows]
    effects[...] = scores[0, rows:]


def total(mine, other, rows):
    sizes = (rows, mine.shape[1] - rows)
    return pl.pallas_call(
        total_kernel,
        out_shape=[jax.ShapeDtypeStruct((size,), jnp.float32) for size in sizes],
        in_specs=[VMEM] * 2,
        out_specs=[VMEM] * 2,
        compiler_params=pltpu.CompilerParams(vmem_limit_bytes=1 << 20),
        name="total",
    )(mine, other)


def gathered_features(tokens, proj, lanes):
    rep, half = lax.axis_index("rep"), lax.axis_index("grp")
    width = proj.shape[2] // lax.axis_size("rep")
    count = sum(piece.shape[0] for piece in tokens)

    def columns(side):
        return jnp.concatenate(
            [lax.dynamic_slice_in_dim(piece, side * width, width, 1) for piece in tokens], 0
        )

    theirs = crossed(columns(1 - rep), "rep", 1)
    panels = lax.all_gather(
        lax.dynamic_slice_in_dim(proj, rep * width, width, 2), "seq", axis=1, tiled=True
    )
    both = jnp.concatenate([columns(rep), theirs], 0)
    partial = jnp.einsum("td,fcd->ftc", both, panels, preferred_element_type=jnp.float32)
    keep = lax.dynamic_slice_in_dim(partial, half * lanes, lanes, 2)
    give = lax.dynamic_slice_in_dim(partial, (1 - half) * lanes, lanes, 2)
    chip = keep + crossed(give, "grp", 1)
    return chip[:, :count], crossed(chip[:, count:], "rep", 1)


def cube_features(tokens, alternates, proj, early):
    width = proj.shape[2] // lax.axis_size("rep")
    bar = lax.optimization_barrier

    own, own_a, own_b = panels(proj, width)
    own_4a = crossed(own_a, "seq", 4)
    own_4b = crossed(own_b, "seq", 4)
    own_2 = crossed(own, "seq", 2)
    own_1 = crossed(own, "seq", 1)
    theirs = crossed(columns(tokens, alternates, width), "rep", 1)
    own_2, own_1, own_4a = bar((own_2, own_1, own_4a))
    own_3 = crossed(own_2, "seq", 1)
    own_4a, own_4b, own_3, early = bar((own_4a, own_4b, own_3, early))
    own_6a = crossed(own_4a, "seq", 2)
    own_6b = crossed(own_4b, "seq", 2)
    own_5b = crossed(own_4b, "seq", 1)
    own_5a = crossed(own_4a, "seq", 1)
    own_6a, own_6b, own_5a, own_5b = bar((own_6a, own_6b, own_5a, own_5b))
    own_7a = crossed(own_6a, "seq", 1)
    own_7b = crossed(own_5b, "seq", 2)

    near = own, own_1, own_2, own_3
    far = own_4a, own_4b, own_5a, own_5b, own_6a, own_6b, own_7a, own_7b
    give_other, keep_other, give_mine, keep_mine = products(tokens, alternates, theirs, near + far)
    other = crossed(keep_other + crossed(give_other, "grp", 1), "rep", 1)
    return (keep_mine, other) + tuple(crossed(part, "grp", 1) for part in give_mine), early


def per_device(hidden, proj, short_taps, filters, grad_out, var_pos, alt_hidden):
    lanes = grad_out.shape[1]
    span = filters.shape[1]
    early = bands(filters), short_taps, var_pos
    if lax.axis_size("seq") == 8:
        terms, early = cube_features(hidden, alt_hidden, proj, early)
    else:
        terms = gathered_features((hidden, alt_hidden), proj, lanes)
    weights, short_taps, picks = early
    feature, within, across = edges(grad_out, short_taps, span, terms)
    within, across = paired(within, "seq", 0), paired(across, "seq", 1)
    scores = mixer(picks, feature, within, across, grad_out, short_taps, span, weights)
    return tuple(total(scores, crossed(scores, "grp", 1), grad_out.shape[0]))


def solution(mesh):
    in_specs = (
        P(("rep", "seq"), "grp"),
        P(None, "seq", "grp"),
        P(None, None, "grp"),
        P("grp", None),
        P(("rep", "seq"), "grp"),
        P(("rep", "seq")),
        P(("rep", "seq"), "grp"),
    )
    out_specs = (P(("rep", "seq")), P(("rep", "seq")))
    return jax.shard_map(
        per_device, mesh=mesh, in_specs=in_specs, out_specs=out_specs, check_vma=False
    )
```

```python
import functools

import jax
import jax.numpy as jnp
from jax import lax
from jax.experimental import pallas as pl
from jax.experimental.pallas import tpu as pltpu
from jax.sharding import PartitionSpec as P

D = 8192
GROUP = 16
EDGE = 8
BAND = 96
PIECES = 2
AXES = ("rep", "seq", "grp")
VMEM = pl.BlockSpec(memory_space=pltpu.VMEM)
ANY = pl.BlockSpec(memory_space=pl.ANY)
HBM = pl.BlockSpec(memory_space=pltpu.HBM)
SMEM = pl.BlockSpec(memory_space=pltpu.SMEM)


def paired(block, axis, first):
    route = []
    for left in range(first, lax.axis_size(axis) - 1, 2):
        route += [(left, left + 1), (left + 1, left)]
    return lax.ppermute(block, axis, route)


def crossed(block, axis, bit):
    return lax.ppermute(block, axis, [(i, i ^ bit) for i in range(lax.axis_size(axis))])


def moved(pairs, sems):
    copies = [
        pltpu.make_async_copy(source, target, sems.at[index])
        for index, (source, target) in enumerate(pairs)
    ]
    for copy in copies:
        copy.start()
    return copies


def part(side, width):
    return pl.ds(pl.multiple_of(side * width, width), width)


def panels_kernel(proj, own, first, second, sems):
    width = own.shape[2]
    cut = first.shape[1]
    home = part(lax.axis_index("rep"), width)
    copies = moved(
        [
            (proj.at[:, :, home], own),
            (proj.at[:, :cut, home], first),
            (proj.at[:, cut:, home], second),
        ],
        sems,
    )
    for copy in copies:
        copy.wait()


def panels(proj, width):
    kinds, height, _ = proj.shape
    shapes = [(kinds, height, width)] + [(kinds, height // 2, width)] * 2
    return pl.pallas_call(
        panels_kernel,
        out_shape=[jax.ShapeDtypeStruct(shape, proj.dtype) for shape in shapes],
        in_specs=[ANY],
        out_specs=[VMEM] * 3,
        scratch_shapes=[pltpu.SemaphoreType.DMA((3,))],
        compiler_params=pltpu.CompilerParams(vmem_limit_bytes=2 << 20),
        name="panels",
    )(proj)


def columns_kernel(tokens, alternates, theirs, sems):
    rows = tokens.shape[0]
    away = part(1 - lax.axis_index("rep"), theirs.shape[1])
    step = rows // PIECES
    copies = moved(
        [(alternates.at[:, away], theirs.at[rows:])]
        + [
            (tokens.at[begin : begin + step, away], theirs.at[begin : begin + step])
            for begin in range(0, rows, step)
        ],
        sems,
    )
    for copy in copies:
        copy.wait()


def columns(tokens, alternates, width):
    count = tokens.shape[0] + alternates.shape[0]
    return pl.pallas_call(
        columns_kernel,
        out_shape=jax.ShapeDtypeStruct((count, width), tokens.dtype),
        in_specs=[ANY] * 2,
        out_specs=VMEM,
        scratch_shapes=[pltpu.SemaphoreType.DMA((1 + PIECES,))],
        compiler_params=pltpu.CompilerParams(vmem_limit_bytes=3 << 20),
        name="columns",
    )(tokens, alternates)


def dots(tokens, panel, side, outs):
    lanes = outs[0].shape[1]
    size = len(outs) * lanes
    result = lax.dot_general(
        tokens[...],
        panel[side * size : (side + 1) * size],
        (((1,), (1,)), ((), ())),
        preferred_element_type=jnp.float32,
    )
    for kind, out in enumerate(outs):
        out[...] = result[:, kind * lanes : (kind + 1) * lanes]


def kinds_of(out):
    return [out.at[kind] for kind in range(out.shape[0])]


def fill(panel, blocks, lanes, done):
    quarter = lanes // 4
    seq = lax.axis_index("seq")
    swap = lax.axis_index("grp") ^ (seq // 4)
    for block in blocks:
        kinds, height, _ = block.shape
        order = done // quarter
        side = ((order // 4) ^ swap) * kinds * lanes
        at = ((seq % 4) ^ (order % 4)) * quarter + done % quarter
        for kind in range(kinds):
            panel[pl.ds(pl.multiple_of(side + kind * lanes + at, 16), height), :] = block[kind]
        done += height


def panel_kernel(lanes, *refs):
    fill(refs[-1], refs[:-1], lanes, 0)


def theirs_kernel(theirs, begun, *refs):
    blocks, (give, panel) = refs[:-2], refs[-2:]
    lanes = give.shape[2]
    fill(panel, blocks, lanes, 2 * lanes - sum(block.shape[1] for block in blocks))
    dots(theirs, panel, 1, kinds_of(give))


def keep_kernel(theirs, panel, keep):
    dots(theirs, panel, 0, kinds_of(keep))


def ours_kernel(tokens, alternates, panel, give_query, give_key, give_value, keep, ours, sems):
    rows = tokens.shape[0]
    home = part(lax.axis_index("rep"), ours.shape[1])
    copies = moved(
        [(tokens.at[:, home], ours.at[:rows]), (alternates.at[:, home], ours.at[rows:])], sems
    )
    for copy in copies:
        copy.wait()
    dots(ours, panel, 1, (give_query, give_key, give_value))
    dots(ours, panel, 0, kinds_of(keep))


def products(tokens, alternates, theirs, blocks):
    count, width = theirs.shape
    kinds = blocks[0].shape[0]
    lanes = sum(block.shape[1] for block in blocks) // 2
    half = jax.ShapeDtypeStruct((kinds, count, lanes), jnp.float32)
    params = pltpu.CompilerParams(vmem_limit_bytes=10 << 20)
    cost = pl.CostEstimate(
        flops=4 * count * kinds * lanes * width,
        bytes_accessed=2 * width * (count + 2 * kinds * lanes) + 8 * kinds * count * lanes,
        transcendentals=0,
    )
    whole = jax.ShapeDtypeStruct((2 * kinds * lanes, width), theirs.dtype)
    first, last = blocks[:-2], blocks[-2:]
    begun = pl.pallas_call(
        functools.partial(panel_kernel, lanes),
        out_shape=whole,
        in_specs=[VMEM] * len(first),
        out_specs=VMEM,
        compiler_params=params,
        name="panel",
    )(*first)
    give_other, panel = pl.pallas_call(
        theirs_kernel,
        out_shape=[half, whole],
        in_specs=[VMEM] * (2 + len(last)),
        out_specs=[VMEM] * 2,
        input_output_aliases={1: 1},
        compiler_params=params,
        cost_estimate=cost,
        name="theirs",
    )(theirs, begun, *last)
    keep_other = pl.pallas_call(
        keep_kernel,
        out_shape=half,
        in_specs=[VMEM] * 2,
        out_specs=VMEM,
        compiler_params=params,
        cost_estimate=cost,
        name="keep",
    )(theirs, panel)
    *give_mine, keep_mine = pl.pallas_call(
        ours_kernel,
        out_shape=[jax.ShapeDtypeStruct((count, lanes), jnp.float32)] * kinds + [half],
        in_specs=[ANY, ANY, VMEM],
        out_specs=[VMEM] * (kinds + 1),
        scratch_shapes=[pltpu.VMEM((count, width), theirs.dtype), pltpu.SemaphoreType.DMA((2,))],
        compiler_params=params,
        cost_estimate=cost,
        name="ours",
    )(tokens, alternates, panel)
    return give_other, keep_other, give_mine, keep_mine


def bands_kernel(filters, *outs):
    groups, span = filters.shape
    deep = 2 * span
    row = lax.broadcasted_iota(jnp.int32, (span, deep), 0)
    column = lax.broadcasted_iota(jnp.int32, (span, deep), 1)
    for later in (False, True):
        place = jnp.where(column == (row if later else span - row), 1.0, 0.0)
        taps = lax.dot_general(
            filters[...],
            place,
            (((1,), (0,)), ((), ())),
            precision=lax.Precision.HIGHEST,
            preferred_element_type=jnp.float32,
        )
        for group in range(groups):
            band = jnp.broadcast_to(taps[group : group + 1], (BAND, deep))
            band = pltpu.roll(band, 0, 1, stride=1, stride_axis=0)
            high = band.astype(jnp.bfloat16)
            at = pl.ds(group * BAND, BAND)
            outs[2 * later][at] = high
            outs[2 * later + 1][at] = (band - high.astype(jnp.float32)).astype(jnp.bfloat16)


def bands(filters):
    groups, span = filters.shape
    return pl.pallas_call(
        bands_kernel,
        out_shape=[jax.ShapeDtypeStruct((groups * BAND, 2 * span), jnp.bfloat16)] * 4,
        in_specs=[VMEM],
        out_specs=[VMEM] * 4,
        compiler_params=pltpu.CompilerParams(vmem_limit_bytes=4 << 20),
        name="bands",
    )(filters)


def tap(taps, offset, index):
    return taps[offset, index : index + 1, :]


def mixed(taps, index, extended, begin, count):
    total = tap(taps, 0, index) * extended[begin : begin + count]
    for offset in (1, 2):
        total = total + tap(taps, offset, index) * extended[begin - offset : begin - offset + count]
    return total


def edges_kernel(span, rows, grad, taps, *refs):
    terms, (feature, within, across, before, after, head) = refs[:-6], refs[-6:]
    for kind in range(3):
        total = terms[0][kind] + terms[1][kind]
        if len(terms) > 2:
            total = total + terms[2 + kind][...]
        feature[kind] = total
    begin = rows - span
    before[:span] = mixed(taps, 1, feature.at[1], begin, span) * mixed(
        taps, 2, feature.at[2], begin, span
    )
    for place, kind in enumerate((1, 2, 0)):
        at = span + place * EDGE
        before[at : at + EDGE] = feature[kind, rows - EDGE : rows]
    before[span + 3 * EDGE :] = jnp.zeros((2 * EDGE, head.shape[1]), jnp.float32)
    reach = span + EDGE
    head[:EDGE] = jnp.zeros((EDGE, head.shape[1]), jnp.float32)
    head[EDGE:] = feature[0, :reach]
    slope = grad[:reach].astype(jnp.float32)
    after[:reach] = slope * mixed(taps, 0, head, EDGE, reach)
    for kind in range(3):
        at = reach + kind * EDGE
        after[at : at + EDGE] = feature[kind, :EDGE]
    after[reach + 3 * EDGE :] = slope[:EDGE]
    even = lax.axis_index("seq") % 2 == 0
    within[...] = jnp.where(even, before[...], after[...])
    across[...] = jnp.where(even, after[...], before[...])


def edges(grad, taps, span, terms):
    rows, lanes = grad.shape
    size = span + 5 * EDGE
    return pl.pallas_call(
        functools.partial(edges_kernel, span, rows),
        out_shape=[jax.ShapeDtypeStruct(terms[0].shape, jnp.float32)]
        + [jax.ShapeDtypeStruct((size, lanes), jnp.float32)] * 2,
        in_specs=[VMEM] * (2 + len(terms)),
        out_specs=[VMEM] * 3,
        scratch_shapes=[pltpu.VMEM((size, lanes), jnp.float32)] * 2
        + [pltpu.VMEM((span + 2 * EDGE, lanes), jnp.float32)],
        compiler_params=pltpu.CompilerParams(vmem_limit_bytes=6 << 20),
        name="edges",
    )(grad, taps, *terms)


def mixer_kernel(
    rows, span, picks, feature, within, across, grad, taps, high, low, later_high, later_low,
    out, before, after, query, key, value, product, back_filtered, filtered,
    back_product, grads, summed,
):
    lanes = grad.shape[1]
    variants = picks.shape[0]
    first = lax.axis_index("seq") * rows
    ahead = rows + EDGE
    reach = span + EDGE
    even = lax.axis_index("seq") % 2 == 0
    before[...] = jnp.where(even, across[...], within[...])
    after[...] = jnp.where(even, within[...], across[...])
    for kind, place, extended in ((1, 0, key), (2, 1, value), (0, 2, query)):
        extended[:EDGE] = before[span + place * EDGE : span + (place + 1) * EDGE]
        extended[EDGE:ahead] = feature[kind, :rows]
        extended[ahead:] = after[reach + kind * EDGE : reach + (kind + 1) * EDGE]
    slope_after = after[reach + 3 * EDGE :]
    key[EDGE:] = mixed(taps, 1, key, EDGE, ahead)
    value[EDGE:] = mixed(taps, 2, value, EDGE, ahead)
    product[:span] = before[:span]
    product[span : span + ahead] = key[EDGE:] * value[EDGE:]
    product[span + ahead :] = jnp.zeros((product.shape[0] - span - ahead, lanes), jnp.float32)
    query[EDGE:] = mixed(taps, 0, query, EDGE, ahead)
    back_filtered[:rows] = grad[...].astype(jnp.float32) * query[EDGE:ahead]
    back_filtered[rows:ahead] = slope_after * query[ahead:]
    back_filtered[ahead : rows + reach] = after[EDGE:reach]
    back_filtered[rows + reach :] = jnp.zeros(
        (back_filtered.shape[0] - rows - reach, lanes), jnp.float32
    )

    owner = lax.broadcasted_iota(jnp.int32, (BAND, lanes), 1) // GROUP

    def long_filter(source, high, low, out):
        for begin in range(0, out.shape[0], BAND):
            section = source[begin : begin + 2 * span]
            upper = section.astype(jnp.bfloat16)
            lower = (section - upper.astype(jnp.float32)).astype(jnp.bfloat16)
            both = jnp.dot(
                high[...], jnp.concatenate([upper, lower], 1), preferred_element_type=jnp.float32
            )
            rest = jnp.dot(low[...], upper, preferred_element_type=jnp.float32)
            summed = both[:, :lanes] + both[:, lanes:] + rest
            chosen = summed[:BAND]
            for group in range(1, lanes // GROUP):
                chosen = jnp.where(
                    owner == group, summed[group * BAND : (group + 1) * BAND], chosen
                )
            out[begin : begin + BAND] = chosen

    long_filter(product, high, low, filtered)
    long_filter(back_filtered, later_high, later_low, back_product)
    grads[0, :rows] = grad[...].astype(jnp.float32) * filtered[:rows]
    grads[0, rows:] = slope_after * filtered[rows:ahead]
    grads[1] = back_product[:ahead] * value[EDGE:]
    grads[2] = back_product[:ahead] * key[EDGE:]
    total = jnp.zeros((rows, lanes), jnp.float32)
    for index in range(3):
        back = tap(taps, 0, index) * grads[index, :rows]
        for offset in (1, 2):
            back = back + tap(taps, offset, index) * grads[index, offset : offset + rows]
        back = back.astype(jnp.bfloat16).astype(jnp.float32)
        grads[index, :rows] = back
        total = total + back * feature[index, :rows]
    summed[:rows] = total
    for variant in range(variants):
        at = picks[variant] - first
        change = jnp.zeros((1, lanes), jnp.float32)
        for index in range(3):
            alternate = feature[index, rows + variant : rows + variant + 1]
            present = feature[index, pl.ds(at, 1)]
            change = change + grads[index, pl.ds(at, 1)] * (alternate - present)
        summed[rows + variant : rows + variant + 1] = change
    scores = lax.dot_general(
        jnp.full((8, lanes), 1.0, jnp.float32),
        summed[...],
        (((1,), (1,)), ((), ())),
        precision=lax.Precision.HIGHEST,
        preferred_element_type=jnp.float32,
    )
    out[...] = scores * D ** (-0.5)


def mixer(picks, feature, within, across, grad, taps, span, weights):
    rows, lanes = grad.shape
    count = feature.shape[1]

    def body(*refs):
        mixer_kernel(rows, span, *refs)

    steps = pl.cdiv(rows + EDGE, BAND)
    length = (steps - 1) * BAND + 2 * span
    return pl.pallas_call(
        body,
        out_shape=jax.ShapeDtypeStruct((8, count), jnp.float32),
        in_specs=[SMEM] + [VMEM] * 9,
        out_specs=VMEM,
        scratch_shapes=[pltpu.VMEM((span + 5 * EDGE, lanes), jnp.float32)] * 2
        + [pltpu.VMEM((rows + 2 * EDGE, lanes), jnp.float32)] * 3
        + [
            pltpu.VMEM((length, lanes), jnp.float32),
            pltpu.VMEM((length, lanes), jnp.float32),
            pltpu.VMEM((steps * BAND, lanes), jnp.float32),
            pltpu.VMEM((steps * BAND, lanes), jnp.float32),
            pltpu.VMEM((3, rows + EDGE, lanes), jnp.float32),
            pltpu.VMEM((count, lanes), jnp.float32),
        ],
        compiler_params=pltpu.CompilerParams(vmem_limit_bytes=12 << 20),
        name="mixer",
    )(picks, feature, within, across, grad, taps, *weights)


def total_kernel(mine, other, out, effects):
    rows = out.shape[0]
    scores = mine[:1] + other[:1]
    out[...] = scores[0, :rows]
    effects[...] = scores[0, rows:]


def total(mine, other, rows):
    sizes = (rows, mine.shape[1] - rows)
    return pl.pallas_call(
        total_kernel,
        out_shape=[jax.ShapeDtypeStruct((size,), jnp.float32) for size in sizes],
        in_specs=[VMEM] * 2,
        out_specs=[VMEM] * 2,
        compiler_params=pltpu.CompilerParams(vmem_limit_bytes=1 << 20),
        name="total",
    )(mine, other)


def gathered_features(tokens, proj, lanes):
    rep, half = lax.axis_index("rep"), lax.axis_index("grp")
    width = proj.shape[2] // lax.axis_size("rep")
    count = sum(piece.shape[0] for piece in tokens)

    def columns(side):
        return jnp.concatenate(
            [lax.dynamic_slice_in_dim(piece, side * width, width, 1) for piece in tokens], 0
        )

    theirs = crossed(columns(1 - rep), "rep", 1)
    panels = lax.all_gather(
        lax.dynamic_slice_in_dim(proj, rep * width, width, 2), "seq", axis=1, tiled=True
    )
    both = jnp.concatenate([columns(rep), theirs], 0)
    partial = jnp.einsum("td,fcd->ftc", both, panels, preferred_element_type=jnp.float32)
    keep = lax.dynamic_slice_in_dim(partial, half * lanes, lanes, 2)
    give = lax.dynamic_slice_in_dim(partial, (1 - half) * lanes, lanes, 2)
    chip = keep + crossed(give, "grp", 1)
    return chip[:, :count], crossed(chip[:, count:], "rep", 1)


def cube_features(tokens, alternates, proj, early):
    width = proj.shape[2] // lax.axis_size("rep")
    bar = lax.optimization_barrier

    own, own_a, own_b = panels(proj, width)
    own_4a = crossed(own_a, "seq", 4)
    own_4b = crossed(own_b, "seq", 4)
    own_2 = crossed(own, "seq", 2)
    own_1 = crossed(own, "seq", 1)
    theirs = crossed(columns(tokens, alternates, width), "rep", 1)
    own_2, own_1, own_4a = bar((own_2, own_1, own_4a))
    own_3 = crossed(own_2, "seq", 1)
    own_4a, own_4b, own_3, early = bar((own_4a, own_4b, own_3, early))
    own_6a = crossed(own_4a, "seq", 2)
    own_6b = crossed(own_4b, "seq", 2)
    own_5b = crossed(own_4b, "seq", 1)
    own_5a = crossed(own_4a, "seq", 1)
    own_6a, own_6b, own_5a, own_5b = bar((own_6a, own_6b, own_5a, own_5b))
    own_7a = crossed(own_6a, "seq", 1)
    own_7b = crossed(own_5b, "seq", 2)

    near = own, own_1, own_2, own_3
    far = own_4a, own_4b, own_5a, own_5b, own_6a, own_6b, own_7a, own_7b
    give_other, keep_other, give_mine, keep_mine = products(tokens, alternates, theirs, near + far)
    other = crossed(keep_other + crossed(give_other, "grp", 1), "rep", 1)
    return (keep_mine, other) + tuple(crossed(part, "grp", 1) for part in give_mine), early


def per_device(hidden, proj, short_taps, filters, grad_out, var_pos, alt_hidden):
    lanes = grad_out.shape[1]
    span = filters.shape[1]
    early = bands(filters), short_taps, var_pos
    if lax.axis_size("seq") == 8:
        terms, early = cube_features(hidden, alt_hidden, proj, early)
    else:
        terms = gathered_features((hidden, alt_hidden), proj, lanes)
    weights, short_taps, picks = early
    feature, within, across = edges(grad_out, short_taps, span, terms)
    within, across = paired(within, "seq", 0), paired(across, "seq", 1)
    scores = mixer(picks, feature, within, across, grad_out, short_taps, span, weights)
    return tuple(total(scores, crossed(scores, "grp", 1), grad_out.shape[0]))


def solution(mesh):
    in_specs = (
        P(("rep", "seq"), "grp"),
        P(None, "seq", "grp"),
        P(None, None, "grp"),
        P("grp", None),
        P(("rep", "seq"), "grp"),
        P(("rep", "seq")),
        P(("rep", "seq"), "grp"),
    )
    out_specs = (P(("rep", "seq")), P(("rep", "seq")))
    return jax.shard_map(
        per_device, mesh=mesh, in_specs=in_specs, out_specs=out_specs, check_vma=False
    )
```
